32 devices in a mesh: ctx: 8 (over z, y), head: 4 (over x, core).
Axes of the slice: x: 2, y: 2, z: 4, core: 2. Of those that a mesh axis runs over, the one named last changes fastest.
Arguments:
- query_all: bfloat16 [1024, 1024], P('ctx', 'head'), may hold values from -6 to 6
- key_all: bfloat16 [1024, 1024], P('ctx', 'head'), may hold values from -6 to 6
- value_all: bfloat16 [1024, 1024], P('ctx', 'head'), may hold values from -6 to 6
- cotangent: bfloat16 [1024, 1024], P('ctx', 'head'), may hold values from -6 to 6
- conv_input: bfloat16 [1024, 1024], P('ctx', 'head'), may hold values from -6 to 6
- rec_lengths: int32 [3], replicated, may hold values from 170 to 341
- out_proj: bfloat16 [1024, 1024], P(None, 'head'), may hold values from -0.1875 to 0.1875
- conv_weight: bfloat16 [31, 1024], P(None, 'head'), may hold values from -1 to 1
Outputs:
- q_grad: bfloat16 [1024, 1024], P('ctx', 'head')
- k_grad: bfloat16 [1024, 1024], P('ctx', 'head')
- v_grad: bfloat16 [1024, 1024], P('ctx', 'head')
- x_grad: bfloat16 [1024, 1024], P('ctx', 'head')
- out_proj_grad: float32 [1024, 1024], P('ctx', 'head')
- conv_weight_grad: float32 [31, 1024], P(None, 'head')
The draws below stay inside these ranges and needn't reach their ends.
Inputs may be any that keep to these rules, and one draw needn't show every extreme that they name: `rec_lengths`: the recordings lie end to end from frame 0; frames from their total on are padding.
All inputs are finite; a program needn't handle non-finite values.
Results may differ from the reference program's by a relative error of at most 0.03.
Values may be sent and summed in bfloat16 or wider, within the bound.
No kernel may reach another device: no remote copies, remote signals or barrier semaphores. Data moves between devices by JAX's collectives and lax.ppermute only.
A program may use at most 64 MiB of HBM per device.

```python
import math
import jax
import jax.numpy as jnp
from jax import lax

HEADS = 16
HEAD_DIM = 64
D = 1024
KW = 31
NREC = 3
FRAMES = 1024


def draw_query_all(key, part):
    values = jnp.clip(1.4 * jax.random.normal(jax.random.fold_in(key, 11), (FRAMES, D), jnp.float32), -6.0, 6.0)
    return values.astype(jnp.bfloat16)


def draw_key_all(key, part):
    values = jnp.clip(1.4 * jax.random.normal(jax.random.fold_in(key, 23), (FRAMES, D), jnp.float32), -6.0, 6.0)
    return values.astype(jnp.bfloat16)


def strengthened(entries, own_key, source, target, shards_of, factor):
    def block_of(dim):
        return (jnp.arange(entries.shape[dim]) // (entries.shape[dim] // shards_of)).reshape((-1,) + (1,) * (entries.ndim - 1 - dim))

    near = jax.random.permutation(own_key, shards_of)[block_of(target)]
    other_side = (block_of(target) + shards_of // 2) % shards_of
    return jnp.where((block_of(source) == near) | (block_of(source) == other_side), factor * entries, entries)


def level_of(key, shape, split, low, high):
    level, own = 1.0, jax.random.fold_in(key, 6)
    for position, parts in split:
        draws = jnp.exp(jax.random.uniform(jax.random.fold_in(own, position), (parts,), jnp.float32, low / len(split), high / len(split)))
        level = level * jnp.repeat(draws, shape[position] // parts).reshape([-1 if axis == position else 1 for axis in range(len(shape))])
    return level


def gaussian(rng, extent, width, most, cuts=(), kind=jnp.bfloat16):
    values = width * jax.random.normal(rng, extent, jnp.float32)
    if cuts:
        values = values * level_of(rng, extent, cuts, -0.22, 0.18)
    return jnp.clip(values, -most, most).astype(kind)


def noise_with(stream_key, extent, scale, most, shards, heavy, kind=jnp.bfloat16):
    array = scale * jax.random.normal(stream_key, extent, jnp.float32)
    if shards:
        array = array * level_of(stream_key, extent, shards, -0.22, 0.18)
    return jnp.clip(strengthened(array, jax.random.fold_in(stream_key, 3), *heavy), -most, most).astype(kind)


def setup_inputs(seed: int = 0) -> dict:
    keys = jax.random.split(jax.random.key(seed), 9)
    query_all = draw_query_all(jax.random.fold_in(keys[8], 71), 0)
    key_all = draw_key_all(jax.random.fold_in(keys[8], 71), 0)
    value_all = gaussian(keys[2], (FRAMES, D), 1.0, 6.0, ((0, 8), (1, 4)))
    cotangent = noise_with(keys[3], (FRAMES, D), 1.0, 6.0, ((0, 8), (1, 4)), (0, 1, 8, 2.0))
    conv_input = gaussian(keys[4], (FRAMES, D), 1.0, 6.0, ((0, 8), (1, 4)))
    rec_lengths = jax.random.randint(keys[5], (NREC,), FRAMES // 6, FRAMES // 3 + 1).astype(jnp.int32)
    out_proj = gaussian(keys[6], (D, D), D ** -0.5, 0.1875, ((1, 4),))
    conv_weight = gaussian(keys[7], (KW, D), KW ** -0.5, 1.0, ((1, 4),))
    return {"query_all": query_all, "key_all": key_all, "value_all": value_all, "cotangent": cotangent, "conv_input": conv_input, "rec_lengths": rec_lengths, "out_proj": out_proj, "conv_weight": conv_weight}


def conv_forward(extended, taps, frames):
    wide = extended.astype(jnp.float32)
    weights = taps.astype(jnp.float32)
    result = jnp.zeros((frames, extended.shape[1]), jnp.float32)
    for offset in range(taps.shape[0]):
        result = result + weights[offset] * wide[offset:offset + frames]
    return result


def conv_backward(grad_ext, taps, frames):
    wide = grad_ext.astype(jnp.float32)
    weights = taps.astype(jnp.float32)
    reach = taps.shape[0] - 1
    result = jnp.zeros((frames, grad_ext.shape[1]), jnp.float32)
    for offset in range(taps.shape[0]):
        result = result + weights[offset] * wide[reach - offset:reach - offset + frames]
    return result


def tap_products(grad_conv, extended):
    frames = grad_conv.shape[0]
    wide = extended.astype(jnp.float32)
    grad_wide = grad_conv.astype(jnp.float32)
    rows_out = [jnp.sum(grad_wide * wide[offset:offset + frames], axis=0) for offset in range(extended.shape[0] - frames + 1)]
    return jnp.stack(rows_out)


def gate_slope(conv_out, upstream):
    sigmoid_value = jax.nn.sigmoid(conv_out)
    return (upstream.astype(jnp.float32) * sigmoid_value * (1.0 + conv_out * (1.0 - sigmoid_value))).astype(jnp.bfloat16)


def reference(query_all, key_all, value_all, cotangent, conv_input, rec_lengths, out_proj, conv_weight):
    half_taps = KW // 2
    score_scale = HEAD_DIM ** -0.5
    valid_total = jnp.sum(rec_lengths)
    positions = jnp.arange(FRAMES, dtype=jnp.int32)
    frame_ok = positions < valid_total
    masked = jnp.where(frame_ok[:, None], conv_input, jnp.zeros_like(conv_input))
    padded_input = jnp.pad(masked, ((half_taps, half_taps), (0, 0)))
    conv_out = conv_forward(padded_input, conv_weight, FRAMES)
    grad_conv = gate_slope(conv_out, cotangent)
    conv_weight_grad = tap_products(grad_conv, padded_input)
    padded_grad = jnp.pad(grad_conv, ((half_taps, half_taps), (0, 0)))
    grad_input = conv_backward(padded_grad, conv_weight, FRAMES)
    x_grad = (cotangent.astype(jnp.float32) + jnp.where(frame_ok[:, None], grad_input, 0.0)).astype(jnp.bfloat16)
    grad_out = jnp.dot(x_grad, out_proj, preferred_element_type=jnp.float32).astype(jnp.bfloat16)

    def per_head(matrix):
        return jnp.transpose(matrix.reshape(FRAMES, HEADS, HEAD_DIM), (1, 0, 2))

    block_rows = math.gcd(FRAMES, 512)
    block_count = FRAMES // block_rows

    def one_head(operands):
        query_head, key_head, value_head, grad_head = operands
        keys32 = key_head.astype(jnp.float32)

        def query_block(running, block_index):
            key_acc, value_acc = running
            first_row = (block_index * block_rows).astype(jnp.int32)
            query_rows = lax.dynamic_slice_in_dim(query_head, first_row, block_rows, 0)
            grad_rows = lax.dynamic_slice_in_dim(grad_head, first_row, block_rows, 0)
            scores = jnp.dot(query_rows, key_head.T, preferred_element_type=jnp.float32) * score_scale
            scores = jnp.where(frame_ok[None, :], scores, -jnp.inf)
            row_max = jnp.max(scores, axis=-1)
            totals = jnp.sum(jnp.exp(scores - row_max[:, None]), axis=-1)
            log_total = row_max + jnp.log(totals)
            probs = jnp.exp(scores - log_total[:, None])
            probs16 = probs.astype(jnp.bfloat16)
            attn_out = jnp.dot(probs16, value_head, preferred_element_type=jnp.float32)
            delta = jnp.sum(grad_rows.astype(jnp.float32) * attn_out, axis=-1)
            slopes = jnp.dot(grad_rows, value_head.T, preferred_element_type=jnp.float32)
            dscores = probs * (slopes - delta[:, None])
            dscores16 = dscores.astype(jnp.bfloat16)
            query_grad = score_scale * jnp.dot(dscores, keys32, precision=lax.Precision.HIGHEST)
            key_acc = key_acc + jnp.dot(dscores16.T, query_rows, preferred_element_type=jnp.float32)
            value_acc = value_acc + jnp.dot(probs16.T, grad_rows, preferred_element_type=jnp.float32)
            return (key_acc, value_acc), (query_grad, attn_out)

        zeros_head = jnp.zeros((FRAMES, HEAD_DIM), jnp.float32)
        sums, blocks_out = lax.scan(query_block, (zeros_head, zeros_head), jnp.arange(block_count, dtype=jnp.int32))
        query_grad = blocks_out[0].reshape(FRAMES, HEAD_DIM)
        attn_out = blocks_out[1].reshape(FRAMES, HEAD_DIM)
        return query_grad, score_scale * sums[0], sums[1], attn_out

    results = lax.map(one_head, (per_head(query_all), per_head(key_all), per_head(value_all), per_head(grad_out)))

    def join_heads(tensor):
        return jnp.transpose(tensor, (1, 0, 2)).reshape(FRAMES, HEADS * HEAD_DIM)

    q_grad = join_heads(results[0]).astype(jnp.bfloat16)
    k_grad = join_heads(results[1]).astype(jnp.bfloat16)
    v_grad = join_heads(results[2]).astype(jnp.bfloat16)
    attn16 = join_heads(results[3]).astype(jnp.bfloat16)
    out_proj_grad = jnp.dot(x_grad.T, attn16, preferred_element_type=jnp.float32)
    return (q_grad, k_grad, v_grad, x_grad, out_proj_grad, conv_weight_grad)
```

```python
import functools

import jax
import jax.numpy as jnp
from jax import lax
from jax.experimental import pallas as pl
from jax.experimental.pallas import tpu as pltpu
from jax.sharding import PartitionSpec as P

HEAD_DIM = 64
HALO_X = 32
HALO_G = 16
BF = jnp.bfloat16
F32 = jnp.float32
VM = pl.BlockSpec(memory_space=pltpu.VMEM)
SM = pl.BlockSpec(memory_space=pltpu.SMEM)


def dot(a, b, dims):
    return lax.dot_general(a, b, (dims, ((), ())), preferred_element_type=F32)


def call(kernel, out_shape, in_specs, args, scratch=(), flops=1 << 20, limit=None):
    one = not isinstance(out_shape, (tuple, list))
    return pl.pallas_call(
        kernel,
        out_shape=out_shape,
        in_specs=in_specs,
        out_specs=VM if one else tuple(VM for _ in out_shape),
        scratch_shapes=list(scratch),
        compiler_params=pltpu.CompilerParams(vmem_limit_bytes=limit),
        cost_estimate=pl.CostEstimate(flops=flops, bytes_accessed=1 << 20, transcendentals=0),
    )(*args)


def shape(dims, dtype):
    return jax.ShapeDtypeStruct(tuple(dims), dtype)


def pack_kernel(q_ref, k_ref, v_ref, o_ref):
    rows = q_ref.shape[0]
    half = rows // 2
    for m in range(o_ref.shape[0]):
        cols = slice(m * HEAD_DIM, (m + 1) * HEAD_DIM)
        o_ref[m, 0:rows, 0:HEAD_DIM] = k_ref[:, cols]
        o_ref[m, 0:rows, HEAD_DIM:] = v_ref[:, cols]
        o_ref[m, rows:, 0:HEAD_DIM] = q_ref[0:half, cols]
        o_ref[m, rows:, HEAD_DIM:] = q_ref[half:, cols]


def conv_kernel(info_ref, x_ref, g_ref, low_ref, high_ref, w_ref, out_ref, tap_ref, xs, gs):
    rows, width = x_ref.shape
    taps = w_ref.shape[0]
    half = taps // 2
    base, total = info_ref[0], info_ref[1]

    def ok(first, count):
        return (first + lax.broadcasted_iota(jnp.int32, (count, width), 0)) < total

    xs[0:HALO_X] = low_ref[0:HALO_X].astype(F32)
    xs[HALO_X : HALO_X + rows] = x_ref[...].astype(F32)
    xs[HALO_X + rows :] = high_ref[0:HALO_X].astype(F32)
    xs[...] = jnp.where(ok(base - HALO_X, rows + 2 * HALO_X), xs[...], 0.0)
    w = w_ref[...].astype(F32)
    wide = rows + 2 * HALO_G
    shift = HALO_X - HALO_G - half
    acc = jnp.zeros((wide, width), F32)
    for j in range(taps):
        acc = acc + w[j : j + 1] * xs[shift + j : shift + j + wide]
    s = jax.nn.sigmoid(acc)
    slope = s * (1.0 + acc * (1.0 - s))
    gs[0:HALO_G] = low_ref[HALO_X:].astype(F32)
    gs[HALO_G : HALO_G + rows] = g_ref[...].astype(F32)
    gs[HALO_G + rows :] = high_ref[HALO_X:].astype(F32)
    gs[...] = (gs[...] * slope).astype(BF).astype(F32)
    acc = jnp.zeros((rows, width), F32)
    for j in range(taps):
        first = HALO_G + half - j
        acc = acc + w[j : j + 1] * gs[first : first + rows]
    out_ref[...] = (g_ref[...].astype(F32) + jnp.where(ok(base, rows), acc, 0.0)).astype(BF)
    mine = gs[HALO_G : HALO_G + rows]
    for j in range(taps):
        first = HALO_X - half + j
        tap_ref[j : j + 1] = jnp.sum(mine * xs[first : first + rows], axis=0, keepdims=True)
    tap_ref[taps:] = jnp.zeros((tap_ref.shape[0] - taps, width), F32)


def spread_kernel(pieces, full_ref, proj_ref, tap_ref, o_ref):
    rows = full_ref.shape[0]
    half = rows // 2
    go = dot(full_ref[...], proj_ref[...], ((1,), (0,))).astype(BF)
    taps = tap_ref[...].astype(BF)
    n_taps = taps.shape[0]
    for m in range(o_ref.shape[0]):
        cols = slice(m * HEAD_DIM, (m + 1) * HEAD_DIM)
        o_ref[m, 0:half, 0:HEAD_DIM] = go[0:half, cols]
        o_ref[m, 0:half, HEAD_DIM:] = go[half:, cols]
        at = half
        for first in pieces[m]:
            o_ref[m, at : at + rows] = full_ref[:, first : first + 128]
            at += rows
        for side in range(taps.shape[1] // 128):
            o_ref[m, at : at + n_taps] = taps[:, side * 128 : (side + 1) * 128]
            at += n_taps


def widened(x, keep_high):
    x = x.reshape(-1, 128).astype(F32)
    turned = pltpu.roll(x, HEAD_DIM, 1)
    lane = lax.broadcasted_iota(jnp.int32, x.shape, 1)
    used = (lane >= HEAD_DIM) if keep_high else (lane < HEAD_DIM)
    first, second = (turned, x) if keep_high else (x, turned)
    return jnp.concatenate([jnp.where(used, first, 0.0), jnp.where(used, second, 0.0)], 0)


def over(count, body):
    if count <= 2:
        for g in range(count):
            body(g)
    else:
        lax.fori_loop(0, count, lambda g, c: (body(g), c)[1], 0)


def key_block(refs, g):
    if len(refs) == 1:
        block = refs[0][g]
    else:
        block = refs[g][:, 0:128, :]
    return block.reshape(-1, 128)


def forward_kernel(n_keys, scale, start_ref, info_ref, got_ref, *rest):
    kv_refs, (p_ref, a_ref, s_ref, m_ref, l_ref, acc_ref) = rest[:n_keys], rest[n_keys:]
    groups, keys, queries = s_ref.shape
    total = info_ref[1]
    rows = got_ref.shape[1] * 2 // 3
    q = (widened(got_ref[:, rows:, :], False) * scale).astype(BF)
    m_ref[...] = jnp.full(m_ref.shape, -1e30, F32)
    l_ref[...] = jnp.zeros(l_ref.shape, F32)
    acc_ref[...] = jnp.zeros(acc_ref.shape, F32)

    def scores(g):
        s = dot(key_block(kv_refs, g), q, ((1,), (1,)))
        pos = start_ref[g] + lax.broadcasted_iota(jnp.int32, s.shape, 0)
        s = jnp.where(pos < total, s, -1e30)
        s_ref[g] = s
        m_ref[...] = jnp.maximum(m_ref[...], jnp.max(s, axis=0, keepdims=True))

    over(groups, scores)

    def weights(g):
        e = jnp.exp(s_ref[g] - m_ref[...])
        s_ref[g] = e
        l_ref[...] += jnp.sum(e, axis=0, keepdims=True)

    over(groups, weights)
    l_ref[...] = 1.0 / l_ref[...]

    def values(g):
        p = (s_ref[g] * l_ref[...]).astype(BF)
        p_ref[g] = p
        acc_ref[...] += dot(key_block(kv_refs, g), p, ((0,), (0,)))

    over(groups, values)
    attn = acc_ref[HEAD_DIM:, :].T.astype(BF)
    half = queries // 2
    for m in range(a_ref.shape[0]):
        a_ref[m, :, 0:HEAD_DIM] = attn[0:half]
        a_ref[m, :, HEAD_DIM:] = attn[half:]


def backward_kernel(n_keys, scale, p_ref, got_ref, spread_ref, *rest):
    kv_refs, (dkv_ref, dq_ref, s_ref, d_ref, acc_ref) = rest[:n_keys], rest[n_keys:]
    groups, keys, queries = s_ref.shape
    rows = got_ref.shape[1] * 2 // 3
    q = (widened(got_ref[:, rows:, :], False) * scale).astype(BF)
    go = widened(spread_ref[:, 0 : rows // 2, :], True).astype(BF)
    d_ref[...] = jnp.zeros(d_ref.shape, F32)
    acc_ref[...] = jnp.zeros(acc_ref.shape, F32)

    def slopes(g):
        s = dot(key_block(kv_refs, g), go, ((1,), (1,)))
        s_ref[g] = s
        d_ref[...] += jnp.sum(s * p_ref[g].astype(F32), axis=0, keepdims=True)

    over(groups, slopes)

    def grads(g):
        p = p_ref[g]
        ds = (p.astype(F32) * (s_ref[g] - d_ref[...])).astype(BF)
        acc_ref[...] += dot(key_block(kv_refs, g), ds, ((0,), (0,)))
        dkv_ref[g] = (dot(ds, q, ((1,), (0,))) + dot(p, go, ((1,), (0,)))).astype(BF)

    over(groups, grads)
    dq = (acc_ref[0:HEAD_DIM, :] * scale).T.astype(BF)
    half = queries // 2
    dq_ref[:, 0:HEAD_DIM] = dq[0:half]
    dq_ref[:, HEAD_DIM:] = dq[half:]


def project_kernel(spread_ref, attn_ref, o_ref, lhs, rhs):
    members, _, _ = spread_ref.shape
    half = attn_ref.shape[1] // members
    rows = 2 * half
    width = lhs.shape[1]
    acc = jnp.zeros((width, rhs.shape[1]), F32)
    for fold in range(2):
        for i in range(members):
            for side in range(width // 128):
                first = half + side * rows + fold * half
                lhs[i * half : (i + 1) * half, side * 128 : (side + 1) * 128] = spread_ref[
                    i, first : first + half, :
                ]
            rhs[:, i * HEAD_DIM : (i + 1) * HEAD_DIM] = attn_ref[
                i, :, fold * HEAD_DIM : (fold + 1) * HEAD_DIM
            ]
        acc = acc + dot(lhs[...], rhs[...], ((0,), (0,)))
    o_ref[...] = acc


def collect_kernel(kv_ref, dq_ref, o_ref):
    members = o_ref.shape[0]
    rows = o_ref.shape[1] * 2 // 3
    half = rows // 2
    total = kv_ref[0].astype(F32)
    for g in range(1, kv_ref.shape[0]):
        total = total + kv_ref[g].astype(F32)
    total = total.astype(BF)
    for m in range(members):
        o_ref[m, 0:rows, :] = total[m * rows : (m + 1) * rows]
        o_ref[m, rows:, :] = dq_ref[m * half : (m + 1) * half, :]


def unpack_kernel(got_ref, q_ref, k_ref, v_ref):
    rows = q_ref.shape[0]
    half = rows // 2
    for m in range(got_ref.shape[0]):
        cols = slice(m * HEAD_DIM, (m + 1) * HEAD_DIM)
        k_ref[:, cols] = got_ref[m, 0:rows, 0:HEAD_DIM]
        v_ref[:, cols] = got_ref[m, 0:rows, HEAD_DIM:]
        q_ref[0:half, cols] = got_ref[m, rows:, 0:HEAD_DIM]
        q_ref[half:, cols] = got_ref[m, rows:, HEAD_DIM:]


def on_device(
    query_all, key_all, value_all, cotangent, conv_input, rec_lengths, out_proj, conv_weight
):
    rows, width = query_all.shape
    half = rows // 2
    members = width // HEAD_DIM
    n_ctx = lax.axis_size("ctx")
    groups = n_ctx // members
    channels = out_proj.shape[0]
    own_rows = channels // n_ctx
    scale = HEAD_DIM**-0.5
    taps = conv_weight.shape[0]
    tap_rows = -(-taps // 16) * 16
    keys = members * rows
    inside = [[g * members + m for m in range(members)] for g in range(groups)]
    across = [[g * members + m for g in range(groups)] for m in range(members)]
    me = lax.axis_index("ctx")
    group = me // members
    total = jnp.sum(rec_lengths)
    info = jnp.stack([me * rows, total]).astype(jnp.int32)

    def swap(x):
        return lax.all_to_all(x, "ctx", 0, 0, axis_index_groups=inside)

    other = [(i, (i + members) % n_ctx) for i in range(n_ctx)]

    def exchange(parts):
        if groups == 2:
            mine = lax.dynamic_index_in_dim(parts, group, 0, keepdims=False)
            theirs = lax.dynamic_index_in_dim(parts, 1 - group, 0, keepdims=False)
            return jnp.stack([mine, lax.ppermute(theirs, "ctx", other)])
        return lax.all_to_all(parts, "ctx", 0, 0, axis_index_groups=across)

    up = [(i, i + 1) for i in range(n_ctx - 1)]
    down = [(i + 1, i) for i in range(n_ctx - 1)]
    low = lax.ppermute(
        jnp.concatenate([conv_input[rows - HALO_X :], cotangent[rows - HALO_G :]], 0), "ctx", up
    )
    high = lax.ppermute(
        jnp.concatenate([conv_input[:HALO_X], cotangent[:HALO_G]], 0), "ctx", down
    )
    packed = call(
        pack_kernel, shape((members, rows + half, 128), BF), [VM] * 3, (query_all, key_all, value_all)
    )
    got = swap(packed)
    own_kv = got[:, :rows]
    if groups == 2:
        kv = (got, lax.ppermute(own_kv, "ctx", other))
        starts = jnp.stack([group, 1 - group]).astype(jnp.int32) * keys
    else:
        kv = (lax.all_gather(own_kv, "ctx", axis_index_groups=across),)
        starts = jnp.arange(groups, dtype=jnp.int32) * keys
    n_keys = len(kv)
    x_grad, tap_part = call(
        conv_kernel,
        (shape((rows, width), BF), shape((tap_rows, width), F32)),
        [SM] + [VM] * 5,
        (info, conv_input, cotangent, low, high, conv_weight),
        scratch=[pltpu.VMEM((rows + 2 * HALO_X, width), F32), pltpu.VMEM((rows + 2 * HALO_G, width), F32)],
    )
    full = lax.all_gather(x_grad, "head", axis=1, tiled=True)
    slot_channels = groups * own_rows
    if own_rows % 128 == 0:
        ordered = full
        pieces = [
            [(g * members + m) * own_rows + b for g in range(groups) for b in range(0, own_rows, 128)]
            for m in range(members)
        ]
        proj = out_proj
    else:

        def in_order(x, dim):
            split = x.shape[:dim] + (groups, members, own_rows) + x.shape[dim + 1 :]
            return jnp.swapaxes(x.reshape(split), dim, dim + 1).reshape(x.shape)

        ordered = in_order(full, 1)
        proj = in_order(out_proj, 0)
        pieces = [list(range(m * slot_channels, (m + 1) * slot_channels, 128)) for m in range(members)]
    slot_rows = half + slot_channels // 128 * rows + tap_rows * (width // 128)
    spread = swap(
        call(
            functools.partial(spread_kernel, pieces),
            shape((members, slot_rows, 128), BF),
            [VM] * 3,
            (ordered, proj, tap_part),
            flops=2 * rows * channels * width,
        )
    )
    queries = members * rows
    big = 60 << 20
    flops = 2 * queries * keys * groups * 128
    probs, attn = call(
        functools.partial(forward_kernel, n_keys, scale),
        (shape((groups, keys, queries), BF), shape((members, queries // 2, 128), BF)),
        [SM, SM, VM] + [VM] * n_keys,
        (starts, info, got) + kv,
        scratch=[
            pltpu.VMEM((groups, keys, queries), F32),
            pltpu.VMEM((1, queries), F32),
            pltpu.VMEM((1, queries), F32),
            pltpu.VMEM((128, queries), F32),
        ],
        flops=2 * flops,
        limit=big,
    )
    attn_all = swap(attn)
    dkv, dq = call(
        functools.partial(backward_kernel, n_keys, scale),
        (shape((groups, keys, 128), BF), shape((queries // 2, 128), BF)),
        [VM] * (3 + n_keys),
        (probs, got, spread) + kv,
        scratch=[
            pltpu.VMEM((groups, keys, queries), F32),
            pltpu.VMEM((1, queries), F32),
            pltpu.VMEM((128, queries), F32),
        ],
        flops=4 * flops,
        limit=big,
    )
    partial = call(
        project_kernel,
        shape((slot_channels, width), F32),
        [VM] * 2,
        (spread, attn_all),
        scratch=[pltpu.VMEM((members * half, slot_channels), BF), pltpu.VMEM((members * half, width), BF)],
        flops=2 * slot_channels * width * queries,
    ).reshape(groups, own_rows, width)
    out_proj_grad = jnp.sum(exchange(partial.astype(BF)).astype(F32), 0)
    tap_sum = jnp.sum(
        spread[:, half + slot_channels // 128 * rows :].astype(F32), 0
    ).astype(BF)
    tap_all = exchange(jnp.broadcast_to(tap_sum, (groups,) + tap_sum.shape)).astype(F32)
    tap_all = jnp.sum(tap_all, 0).reshape(width // 128, tap_rows, 128)
    conv_weight_grad = jnp.swapaxes(tap_all, 0, 1).reshape(tap_rows, width)[:taps]
    if groups == 2:
        parts = jnp.stack([dkv[0], lax.ppermute(dkv[1], "ctx", other)])
    else:
        parts = exchange(dkv)
    back = swap(
        call(collect_kernel, shape((members, rows + half, 128), BF), [VM] * 2, (parts, dq))
    )
    q_grad, k_grad, v_grad = call(
        unpack_kernel, (shape((rows, width), BF),) * 3, [VM], (back,)
    )
    return (q_grad, k_grad, v_grad, x_grad, out_proj_grad, conv_weight_grad)


def solution(mesh):
    placed = (
        P("ctx", "head"),
        P("ctx", "head"),
        P("ctx", "head"),
        P("ctx", "head"),
        P("ctx", "head"),
        P(),
        P(None, "head"),
        P(None, "head"),
    )
    return jax.shard_map(
        on_device,
        mesh=mesh,
        in_specs=placed,
        out_specs=(
            P("ctx", "head"),
            P("ctx", "head"),
            P("ctx", "head"),
            P("ctx", "head"),
            P("ctx", "head"),
            P(None, "head"),
        ),
        check_vma=False,
    )
```

```python
import functools

import jax
import jax.numpy as jnp
from jax import lax
from jax.experimental import pallas as pl
from jax.experimental.pallas import tpu as pltpu
from jax.sharding import PartitionSpec as P

HEAD_DIM = 64
HALO_X = 32
HALO_G = 16
BF = jnp.bfloat16
F32 = jnp.float32
VM = pl.BlockSpec(memory_space=pltpu.VMEM)
SM = pl.BlockSpec(memory_space=pltpu.SMEM)


def dot(a, b, dims):
    return lax.dot_general(a, b, (dims, ((), ())), preferred_element_type=F32)


def call(kernel, out_shape, args, smem=0, scratch=(), flops=1 << 20, limit=None):
    one = not isinstance(out_shape, (tuple, list))
    return pl.pallas_call(
        kernel,
        out_shape=out_shape,
        in_specs=[SM] * smem + [VM] * (len(args) - smem),
        out_specs=VM if one else tuple(VM for _ in out_shape),
        scratch_shapes=list(scratch),
        compiler_params=pltpu.CompilerParams(vmem_limit_bytes=limit),
        cost_estimate=pl.CostEstimate(flops=flops, bytes_accessed=1 << 20, transcendentals=0),
    )(*args)


def shape(dims, dtype):
    return jax.ShapeDtypeStruct(tuple(dims), dtype)


def member(members):
    return lax.rem(lax.axis_index("ctx"), members)


def total_of(lengths_ref):
    total = lengths_ref[0]
    for i in range(1, lengths_ref.shape[0]):
        total = total + lengths_ref[i]
    return total


def halo_kernel(x_ref, g_ref, up_ref, down_ref):
    rows = x_ref.shape[0]
    up_ref[0:HALO_X] = x_ref[rows - HALO_X :]
    up_ref[HALO_X:] = g_ref[rows - HALO_G :]
    down_ref[0:HALO_X] = x_ref[0:HALO_X]
    down_ref[HALO_X:] = g_ref[0:HALO_G]


def pack_kernel(q_ref, k_ref, v_ref, *rest):
    slots, buf = rest[:-1], rest[-1]
    members = len(slots)
    rows = q_ref.shape[0]
    half = rows // 2
    for m in range(members):
        cols = slice(m * HEAD_DIM, (m + 1) * HEAD_DIM)
        buf[m, 0:rows, 0:HEAD_DIM] = k_ref[:, cols]
        buf[m, 0:rows, HEAD_DIM:] = v_ref[:, cols]
        buf[m, rows:, 0:HEAD_DIM] = q_ref[0:half, cols]
        buf[m, rows:, HEAD_DIM:] = q_ref[half:, cols]
    me = member(members)
    for k in range(members):
        slots[k][...] = buf[me ^ k]


def masked_into(xs, len_ref, x_ref, low_ref, high_ref):
    rows = x_ref.shape[0]
    base = lax.axis_index("ctx") * rows - HALO_X
    total = total_of(len_ref)
    xs[0:HALO_X] = low_ref[0:HALO_X].astype(F32)
    xs[HALO_X : HALO_X + rows] = x_ref[...].astype(F32)
    xs[HALO_X + rows :] = high_ref[0:HALO_X].astype(F32)

    @pl.when(base + xs.shape[0] > total)
    def _():
        pos = base + lax.broadcasted_iota(jnp.int32, xs.shape, 0)
        xs[...] = jnp.where(pos < total, xs[...], 0.0)


def conv_kernel(len_ref, x_ref, g_ref, low_ref, high_ref, w_ref, out_ref, mine_ref, xs, gs):
    rows, width = x_ref.shape
    taps = w_ref.shape[0]
    half = taps // 2
    masked_into(xs, len_ref, x_ref, low_ref, high_ref)
    w = w_ref[...].astype(F32)
    wide = rows + 2 * HALO_G
    shift = HALO_X - HALO_G - half
    acc = jnp.zeros((wide, width), F32)
    for j in range(taps):
        acc = acc + w[j : j + 1] * xs[shift + j : shift + j + wide]
    s = jax.nn.sigmoid(acc)
    slope = s * (1.0 + acc * (1.0 - s))
    gs[0:HALO_G] = low_ref[HALO_X:].astype(F32)
    gs[HALO_G : HALO_G + rows] = g_ref[...].astype(F32)
    gs[HALO_G + rows :] = high_ref[HALO_X:].astype(F32)
    gs[...] = (gs[...] * slope).astype(BF).astype(F32)
    acc = jnp.zeros((rows, width), F32)
    for j in range(taps):
        first = HALO_G + half - j
        acc = acc + w[j : j + 1] * gs[first : first + rows]
    pos = lax.axis_index("ctx") * rows + lax.broadcasted_iota(jnp.int32, acc.shape, 0)
    acc = jnp.where(pos < total_of(len_ref), acc, 0.0)
    out_ref[...] = (g_ref[...].astype(F32) + acc).astype(BF)
    mine_ref[...] = gs[HALO_G : HALO_G + rows].astype(BF)


def taps_kernel(taps, len_ref, x_ref, low_ref, high_ref, mine_ref, tap_ref, xs):
    rows, width = x_ref.shape
    half = taps // 2
    sides = width // 128
    tap_rows = tap_ref.shape[0] // sides
    masked_into(xs, len_ref, x_ref, low_ref, high_ref)
    mine = mine_ref[...].astype(F32)
    sums = []
    for j in range(taps):
        first = HALO_X - half + j
        sums.append(jnp.sum(mine * xs[first : first + rows], axis=0, keepdims=True))
    sums.append(jnp.zeros((tap_rows - taps, width), F32))
    out = jnp.concatenate(sums, 0).astype(BF)
    for side in range(sides):
        tap_ref[side * tap_rows : (side + 1) * tap_rows] = out[:, side * 128 : (side + 1) * 128]


def spread_kernel(pieces, members, proj_ref, *rest):
    n_heads = len(rest) - members - 4
    xs, go_refs = rest[:n_heads], rest[n_heads : n_heads + members]
    piece_ref, full, go_buf, piece_buf = rest[n_heads + members :]
    rows, width = xs[0].shape
    half = rows // 2
    mine = lax.axis_index("head")
    for k in range(n_heads):
        full[mine ^ k] = xs[k][...]
    go = jnp.zeros((rows, proj_ref.shape[1]), F32)
    for b in range(n_heads):
        go = go + dot(full[b], proj_ref[b * width : (b + 1) * width], ((1,), (0,)))
    go = go.astype(BF)
    for m in range(members):
        cols = slice(m * HEAD_DIM, (m + 1) * HEAD_DIM)
        go_buf[m, :, 0:HEAD_DIM] = go[0:half, cols]
        go_buf[m, :, HEAD_DIM:] = go[half:, cols]
        for i, first in enumerate(pieces[m]):
            piece_buf[m, i * rows : (i + 1) * rows] = full[first // width][
                :, first % width : first % width + 128
            ]
    me = member(members)
    for k in range(members):
        go_refs[k][...] = go_buf[me ^ k]
        piece_ref[k] = piece_buf[me ^ k]


def widened(x, keep_high):
    x = x.astype(F32)
    turned = pltpu.roll(x, HEAD_DIM, 1)
    lane = lax.broadcasted_iota(jnp.int32, x.shape, 1)
    used = (lane >= HEAD_DIM) if keep_high else (lane < HEAD_DIM)
    first, second = (turned, x) if keep_high else (x, turned)
    return jnp.concatenate([jnp.where(used, first, 0.0), jnp.where(used, second, 0.0)], 0)


def over(count, body):
    if count <= 2:
        for g in range(count):
            body(g)
    else:
        lax.fori_loop(0, count, lambda g, c: (body(g), c)[1], 0)


def key_block(refs, g):
    return refs[0][g] if len(refs) == 1 else refs[g][...]


def queries_of(got_refs, scale):
    rows = got_refs[0].shape[0] * 2 // 3
    q = jnp.concatenate([r[rows:, :] for r in got_refs], 0)
    return (widened(q, False) * scale).astype(BF)


def forward_kernel(n_keys, members, scale, len_ref, piece_ref, tap_ref, *rest):
    got, rest = rest[:members], rest[members:]
    kv, rest = rest[:n_keys], rest[n_keys:]
    p_ref, slots, (s_ref, m_ref, l_ref, acc_ref) = rest[0], rest[1 : 1 + members], rest[1 + members :]
    groups, keys, queries = s_ref.shape
    rows = keys // members
    total = total_of(len_ref)
    ctx = lax.axis_index("ctx")
    me, group = lax.rem(ctx, members), lax.div(ctx, members)
    q = queries_of(got, scale)
    m_ref[...] = jnp.full(m_ref.shape, -1e30, F32)
    l_ref[...] = jnp.zeros(l_ref.shape, F32)
    acc_ref[...] = jnp.zeros(acc_ref.shape, F32)

    def scores(g):
        s = dot(key_block(kv, g), q, ((1,), (1,)))
        start = (lax.rem(group + g, groups) if n_keys > 1 else g) * keys
        s_ref[g] = s

        @pl.when(start + keys > total)
        def _():
            for k in range(members):
                pos = start + (me ^ k) * rows + lax.broadcasted_iota(jnp.int32, (rows, queries), 0)
                part = s_ref[g, k * rows : (k + 1) * rows]
                s_ref[g, k * rows : (k + 1) * rows] = jnp.where(pos < total, part, -1e30)

        m_ref[...] = jnp.maximum(m_ref[...], jnp.max(s_ref[g], axis=0, keepdims=True))

    over(groups, scores)

    def weights(g):
        e = jnp.exp(s_ref[g] - m_ref[...])
        s_ref[g] = e
        l_ref[...] += jnp.sum(e, axis=0, keepdims=True)

    over(groups, weights)
    l_ref[...] = 1.0 / l_ref[...]

    def values(g):
        p = (s_ref[g] * l_ref[...]).astype(BF)
        p_ref[g] = p
        acc_ref[...] += dot(key_block(kv, g), p, ((0,), (0,)))

    over(groups, values)
    attn = acc_ref[HEAD_DIM:, :].T.astype(BF)
    half = queries // 2
    count = piece_ref.shape[1]
    for k in range(members):
        slots[k][0:count] = piece_ref[k]
        slots[k][count : count + half, 0:HEAD_DIM] = attn[0:half]
        slots[k][count : count + half, HEAD_DIM:] = attn[half:]
        slots[k][count + half :] = tap_ref[...]


def backward_kernel(n_keys, members, scale, p_ref, *rest):
    got, rest = rest[:members], rest[members:]
    gos, rest = rest[:members], rest[members:]
    kv, rest = rest[:n_keys], rest[n_keys:]
    dkv, (dq_ref, s_ref, d_ref, acc_ref) = rest[:n_keys], rest[n_keys:]
    groups, keys, queries = s_ref.shape
    q = queries_of(got, scale)
    go = widened(jnp.concatenate([r[...] for r in gos], 0), True).astype(BF)
    d_ref[...] = jnp.zeros(d_ref.shape, F32)
    acc_ref[...] = jnp.zeros(acc_ref.shape, F32)

    def slopes(g):
        s = dot(key_block(kv, g), go, ((1,), (1,)))
        s_ref[g] = s
        d_ref[...] += jnp.sum(s * p_ref[g].astype(F32), axis=0, keepdims=True)

    over(groups, slopes)

    def grads(g):
        p = p_ref[g]
        ds = (p.astype(F32) * (s_ref[g] - d_ref[...])).astype(BF)
        acc_ref[...] += dot(key_block(kv, g), ds, ((0,), (0,)))
        out = (dot(ds, q, ((1,), (0,))) + dot(p, go, ((1,), (0,)))).astype(BF)
        if n_keys > 1:
            dkv[g][...] = out
        else:
            dkv[0][g] = out

    over(groups, grads)
    dq = (acc_ref[0:HEAD_DIM, :] * scale).T.astype(BF)
    half = queries // 2
    dq_ref[:, 0:HEAD_DIM] = dq[0:half]
    dq_ref[:, HEAD_DIM:] = dq[half:]


def project_kernel(tap_rows, *refs):
    members = len(refs) - 5
    slots, (out_ref, tap_ref, lhs, rhs, heads) = refs[:members], refs[members:]
    count, width = lhs.shape[1], rhs.shape[1]
    half = lhs.shape[0] // members
    rows = 2 * half
    me = member(members)
    first = count // 128 * rows
    acc = jnp.zeros((count, width), F32)
    tap = jnp.zeros((slots[0].shape[0] - first - members * half, 128), F32)
    for k in range(members):
        heads[me ^ k] = slots[k][first : first + members * half]
        tap = tap + slots[k][first + members * half :].astype(F32)
    tap_ref[...] = tap.astype(BF)
    for fold in range(2):
        for k in range(members):
            for side in range(count // 128):
                at = side * rows + fold * half
                where = pl.multiple_of((me ^ k) * half, half)
                lhs[pl.ds(where, half), side * 128 : (side + 1) * 128] = slots[k][at : at + half]
        for h in range(members):
            for i in range(members):
                j = h ^ i
                rhs[i * half : (i + 1) * half, h * HEAD_DIM : (h + 1) * HEAD_DIM] = heads[
                    h, j * half : (j + 1) * half, fold * HEAD_DIM : (fold + 1) * HEAD_DIM
                ]
        acc = acc + dot(lhs[...], rhs[...], ((0,), (0,)))
    out_ref[...] = acc


def collect_kernel(members, *refs):
    parts, dq_ref, slots = refs[: -1 - members], refs[-1 - members], refs[-members:]
    rows = slots[0].shape[0] * 2 // 3
    half = rows // 2
    if len(parts) == 1:
        total = parts[0][0].astype(F32)
        for g in range(1, parts[0].shape[0]):
            total = total + parts[0][g].astype(F32)
    else:
        total = parts[0][...].astype(F32) + parts[1][...].astype(F32)
    total = total.astype(BF)
    for k in range(members):
        slots[k][0:rows] = total[k * rows : (k + 1) * rows]
        slots[k][rows:] = dq_ref[k * half : (k + 1) * half]


def unpack_kernel(*refs):
    members = len(refs) - 4
    slots, (q_ref, k_ref, v_ref, buf) = refs[:members], refs[members:]
    rows = q_ref.shape[0]
    half = rows // 2
    me = member(members)
    for k in range(members):
        buf[me ^ k] = slots[k][...]
    for m in range(members):
        cols = slice(m * HEAD_DIM, (m + 1) * HEAD_DIM)
        k_ref[:, cols] = buf[m, 0:rows, 0:HEAD_DIM]
        v_ref[:, cols] = buf[m, 0:rows, HEAD_DIM:]
        q_ref[0:half, cols] = buf[m, rows:, 0:HEAD_DIM]
        q_ref[half:, cols] = buf[m, rows:, HEAD_DIM:]


def split_kernel(own_rows, part_ref, tap_ref, mine_ref, send_ref):
    group = lax.div(lax.axis_index("ctx"), lax.axis_size("ctx") // 2)
    width = part_ref.shape[1]
    mine_ref[...] = part_ref[pl.ds(pl.multiple_of(group * own_rows, own_rows), own_rows), :]
    theirs = part_ref[pl.ds(pl.multiple_of((1 - group) * own_rows, own_rows), own_rows), :].astype(BF)
    for side in range(width // 128):
        send_ref[side * own_rows : (side + 1) * own_rows] = theirs[:, side * 128 : (side + 1) * 128]
    send_ref[width // 128 * own_rows :] = tap_ref[...]


def finish_kernel(mine_ref, tap_ref, got_ref, out_ref, grad_ref):
    own_rows, width = mine_ref.shape
    taps = grad_ref.shape[0]
    sides = width // 128
    tap_rows = tap_ref.shape[0] // sides
    tap = tap_ref[...].astype(F32) + got_ref[sides * own_rows :].astype(F32)
    for side in range(sides):
        cols = slice(side * 128, (side + 1) * 128)
        out_ref[:, cols] = mine_ref[:, cols] + got_ref[
            side * own_rows : (side + 1) * own_rows
        ].astype(F32)
        grad_ref[:, cols] = tap[side * tap_rows : side * tap_rows + taps]


def on_device(
    query_all, key_all, value_all, cotangent, conv_input, rec_lengths, out_proj, conv_weight
):
    rows, width = query_all.shape
    half = rows // 2
    members = width // HEAD_DIM
    n_ctx, n_heads = lax.axis_size("ctx"), lax.axis_size("head")
    groups = n_ctx // members
    channels = out_proj.shape[0]
    own_rows = channels // n_ctx
    scale = HEAD_DIM**-0.5
    taps = conv_weight.shape[0]
    tap_rows = -(-taps // 16) * 16
    sides = width // 128
    keys = members * rows
    queries = members * rows
    pair = groups == 2
    across = [[g * members + m for g in range(groups)] for m in range(members)]
    other = [(i, (i + members) % n_ctx) for i in range(n_ctx)]

    def swap(slots, axis="ctx"):
        n = lax.axis_size(axis)
        return [slots[0]] + [
            lax.ppermute(slots[k], axis, [(i, i ^ k) for i in range(n)]) for k in range(1, len(slots))
        ]

    up, down = call(
        halo_kernel, (shape((HALO_X + HALO_G, width), BF),) * 2, (conv_input, cotangent)
    )
    low = lax.ppermute(up, "ctx", [(i, i + 1) for i in range(n_ctx - 1)])
    high = lax.ppermute(down, "ctx", [(i + 1, i) for i in range(n_ctx - 1)])
    slot = shape((rows + half, 128), BF)
    got = swap(
        call(
            pack_kernel,
            (slot,) * members,
            (query_all, key_all, value_all),
            scratch=[pltpu.VMEM((members, rows + half, 128), BF)],
        )
    )
    own_kv = jnp.concatenate([x[:rows] for x in got], 0)
    if pair:
        kv = (own_kv, lax.ppermute(own_kv, "ctx", other))
    else:
        kv = (lax.all_gather(own_kv, "ctx", axis_index_groups=across),)
    n_keys = len(kv)
    x_grad, grad_conv = call(
        conv_kernel,
        (shape((rows, width), BF),) * 2,
        (rec_lengths, conv_input, cotangent, low, high, conv_weight),
        smem=1,
        scratch=[
            pltpu.VMEM((rows + 2 * HALO_X, width), F32),
            pltpu.VMEM((rows + 2 * HALO_G, width), F32),
        ],
    )
    xs = swap([x_grad] * n_heads, "head")
    tap_part = call(
        functools.partial(taps_kernel, taps),
        shape((sides * tap_rows, 128), BF),
        (rec_lengths, conv_input, low, high, grad_conv),
        smem=1,
        scratch=[pltpu.VMEM((rows + 2 * HALO_X, width), F32)],
    )
    count = groups * own_rows
    if own_rows % 128 == 0:
        pieces = [
            [(g * members + m) * own_rows + b for g in range(groups) for b in range(0, own_rows, 128)]
            for m in range(members)
        ]
    else:
        pieces = [list(range(m * count, (m + 1) * count, 128)) for m in range(members)]
    spread = call(
        functools.partial(spread_kernel, pieces, members),
        (shape((half, 128), BF),) * members + (shape((members, count // 128 * rows, 128), BF),),
        (out_proj, *xs),
        scratch=[
            pltpu.VMEM((n_heads, rows, width), BF),
            pltpu.VMEM((members, half, 128), BF),
            pltpu.VMEM((members, count // 128 * rows, 128), BF),
        ],
        flops=2 * rows * channels * width,
    )
    piece = spread[members]
    gos = swap(spread[:members])
    big = 60 << 20
    flops = 2 * queries * keys * groups * 128
    fwd = call(
        functools.partial(forward_kernel, n_keys, members, scale),
        (shape((groups, keys, queries), BF),)
        + (shape((count // 128 * rows + queries // 2 + sides * tap_rows, 128), BF),) * members,
        (rec_lengths, piece, tap_part, *got, *kv),
        smem=1,
        scratch=[
            pltpu.VMEM((groups, keys, queries), F32),
            pltpu.VMEM((1, queries), F32),
            pltpu.VMEM((1, queries), F32),
            pltpu.VMEM((128, queries), F32),
        ],
        flops=2 * flops,
        limit=big,
    )
    probs = fwd[0]
    bwd = call(
        functools.partial(backward_kernel, n_keys, members, scale),
        (
            (shape((keys, 128), BF),) * 2
            if pair
            else (shape((groups, keys, 128), BF),)
        )
        + (shape((queries // 2, 128), BF),),
        (probs, *got, *gos, *kv),
        scratch=[
            pltpu.VMEM((groups, keys, queries), F32),
            pltpu.VMEM((1, queries), F32),
            pltpu.VMEM((128, queries), F32),
        ],
        flops=4 * flops,
        limit=big,
    )
    dq = bwd[-1]
    if pair:
        parts = (bwd[0], lax.ppermute(bwd[1], "ctx", other))
    else:
        parts = (lax.all_to_all(bwd[0], "ctx", 0, 0, axis_index_groups=across),)
    back = swap(call(functools.partial(collect_kernel, members), (slot,) * members, (*parts, dq)))
    q_grad, k_grad, v_grad = call(
        unpack_kernel,
        (shape((rows, width), BF),) * 3,
        tuple(back),
        scratch=[pltpu.VMEM((members, rows + half, 128), BF)],
    )
    shared = swap(fwd[1:])
    partial, tap_sum = call(
        functools.partial(project_kernel, tap_rows),
        (shape((count, width), F32), shape((sides * tap_rows, 128), BF)),
        tuple(shared),
        scratch=[
            pltpu.VMEM((members * half, count), BF),
            pltpu.VMEM((members * half, width), BF),
            pltpu.VMEM((members, queries // 2, 128), BF),
        ],
        flops=2 * count * width * queries,
    )
    grads = (shape((own_rows, width), F32), shape((taps, width), F32))
    if pair and own_rows % 16 == 0:
        mine, send = call(
            functools.partial(split_kernel, own_rows),
            (shape((own_rows, width), F32), shape((sides * (own_rows + tap_rows), 128), BF)),
            (partial, tap_sum),
        )
        out_proj_grad, conv_weight_grad = call(
            finish_kernel, grads, (mine, tap_sum, lax.ppermute(send, "ctx", other))
        )
    else:
        if own_rows % 128:
            wanted = partial.astype(BF).reshape(1, groups, own_rows, width)
            slots = jnp.zeros((members, groups, own_rows, width), BF)
            slots = lax.dynamic_update_slice(
                slots, wanted, (lax.rem(lax.axis_index("ctx"), members), 0, 0, 0)
            )
            moved = lax.all_to_all(slots.reshape(n_ctx, own_rows, width), "ctx", 0, 0)
        else:
            moved = lax.all_to_all(
                partial.astype(BF).reshape(groups, own_rows, width),
                "ctx",
                0,
                0,
                axis_index_groups=across,
            )
        out_proj_grad = jnp.sum(moved.astype(F32), 0)
        tap_all = jnp.sum(
            lax.all_gather(tap_sum, "ctx", axis_index_groups=across).astype(F32), 0
        ).reshape(sides, tap_rows, 128)
        conv_weight_grad = jnp.swapaxes(tap_all, 0, 1).reshape(tap_rows, width)[:taps]
    return (q_grad, k_grad, v_grad, x_grad, out_proj_grad, conv_weight_grad)


def solution(mesh):
    placed = (
        P("ctx", "head"),
        P("ctx", "head"),
        P("ctx", "head"),
        P("ctx", "head"),
        P("ctx", "head"),
        P(),
        P(None, "head"),
        P(None, "head"),
    )
    return jax.shard_map(
        on_device,
        mesh=mesh,
        in_specs=placed,
        out_specs=(
            P("ctx", "head"),
            P("ctx", "head"),
            P("ctx", "head"),
            P("ctx", "head"),
            P("ctx", "head"),
            P(None, "head"),
        ),
        check_vma=False,
    )
```

```python
import functools

import jax
import jax.numpy as jnp
from jax import lax
from jax.experimental import pallas as pl
from jax.experimental.pallas import tpu as pltpu
from jax.sharding import PartitionSpec as P


HEAD_DIM = 64
HALO_X = 32
HALO_G = 16
BF = jnp.bfloat16
F32 = jnp.float32
VM = pl.BlockSpec(memory_space=pltpu.VMEM)
SM = pl.BlockSpec(memory_space=pltpu.SMEM)


def dot(a, b, dims):
    return lax.dot_general(a, b, (dims, ((), ())), preferred_element_type=F32)


def call(kernel, out_shape, args, smem=0, scratch=(), flops=1 << 20, limit=None):
    one = not isinstance(out_shape, (tuple, list))
    return pl.pallas_call(
        kernel,
        out_shape=out_shape,
        in_specs=[SM] * smem + [VM] * (len(args) - smem),
        out_specs=VM if one else tuple(VM for _ in out_shape),
        scratch_shapes=list(scratch),
        compiler_params=pltpu.CompilerParams(vmem_limit_bytes=limit or (4 << 20)),
        cost_estimate=pl.CostEstimate(flops=flops, bytes_accessed=1 << 20, transcendentals=0),
    )(*args)


def shape(dims, dtype):
    return jax.ShapeDtypeStruct(tuple(dims), dtype)


def member(members):
    return lax.rem(lax.axis_index("ctx"), members)


def total_of(lengths_ref):
    total = lengths_ref[0]
    for i in range(1, lengths_ref.shape[0]):
        total = total + lengths_ref[i]
    return total


def halo_kernel(x_ref, g_ref, up_ref, down_ref):
    rows = x_ref.shape[0]
    up_ref[0:HALO_X] = x_ref[rows - HALO_X :]
    up_ref[HALO_X:] = g_ref[rows - HALO_G :]
    down_ref[0:HALO_X] = x_ref[0:HALO_X]
    down_ref[HALO_X:] = g_ref[0:HALO_G]


def pack_kernel(q_ref, k_ref, v_ref, after_ref, *rest):
    slots, buf = rest[:-1], rest[-1]
    members = len(slots)
    rows = q_ref.shape[0]
    half = rows // 2
    for m in range(members):
        cols = slice(m * HEAD_DIM, (m + 1) * HEAD_DIM)
        buf[m, 0:rows, 0:HEAD_DIM] = k_ref[:, cols]
        buf[m, 0:rows, HEAD_DIM:] = v_ref[:, cols]
        buf[m, rows:, 0:HEAD_DIM] = q_ref[0:half, cols]
        buf[m, rows:, HEAD_DIM:] = q_ref[half:, cols]
    me = member(members)
    for k in range(members):
        slots[k][...] = buf[me ^ k]


def join_kernel(after_ref, *refs):
    out_ref = refs[-1]
    rows = out_ref.shape[0] // (len(refs) - 1)
    for k, ref in enumerate(refs[:-1]):
        out_ref[k * rows : (k + 1) * rows] = ref[0:rows]


def masked_into(xs, len_ref, x_ref, low_ref, high_ref):
    rows = x_ref.shape[0]
    base = lax.axis_index("ctx") * rows - HALO_X
    total = total_of(len_ref)
    xs[0:HALO_X] = low_ref[0:HALO_X].astype(F32)
    xs[HALO_X : HALO_X + rows] = x_ref[...].astype(F32)
    xs[HALO_X + rows :] = high_ref[0:HALO_X].astype(F32)

    @pl.when(base + xs.shape[0] > total)
    def _():
        pos = base + lax.broadcasted_iota(jnp.int32, xs.shape, 0)
        xs[...] = jnp.where(pos < total, xs[...], 0.0)


def conv_kernel(
    len_ref, x_ref, g_ref, low_ref, high_ref, w_ref, out_ref, send_ref, mine_ref, xs, gs
):
    rows, width = x_ref.shape
    taps = w_ref.shape[0]
    half = taps // 2
    masked_into(xs, len_ref, x_ref, low_ref, high_ref)
    w = w_ref[...].astype(F32)
    wide = rows + 2 * HALO_G
    shift = HALO_X - HALO_G - half
    acc = jnp.zeros((wide, width), F32)
    for j in range(taps):
        acc = acc + w[j : j + 1] * xs[shift + j : shift + j + wide]
    s = jax.nn.sigmoid(acc)
    slope = s * (1.0 + acc * (1.0 - s))
    gs[0:HALO_G] = low_ref[HALO_X:].astype(F32)
    gs[HALO_G : HALO_G + rows] = g_ref[...].astype(F32)
    gs[HALO_G + rows :] = high_ref[HALO_X:].astype(F32)
    gs[...] = (gs[...] * slope).astype(BF).astype(F32)
    acc = jnp.zeros((rows, width), F32)
    for j in range(taps):
        first = HALO_G + half - j
        acc = acc + w[j : j + 1] * gs[first : first + rows]
    pos = lax.axis_index("ctx") * rows + lax.broadcasted_iota(jnp.int32, acc.shape, 0)
    acc = jnp.where(pos < total_of(len_ref), acc, 0.0)
    out = (g_ref[...].astype(F32) + acc).astype(BF)
    out_ref[...] = out
    send_ref[...] = out
    mine_ref[...] = gs[HALO_G : HALO_G + rows].astype(BF)


def taps_kernel(taps, len_ref, x_ref, low_ref, high_ref, mine_ref, tap_ref, xs):
    rows, width = x_ref.shape
    half = taps // 2
    sides = width // 128
    tap_rows = tap_ref.shape[0] // sides
    masked_into(xs, len_ref, x_ref, low_ref, high_ref)
    mine = mine_ref[...].astype(F32)
    sums = []
    for j in range(taps):
        first = HALO_X - half + j
        sums.append(jnp.sum(mine * xs[first : first + rows], axis=0, keepdims=True))
    sums.append(jnp.zeros((tap_rows - taps, width), F32))
    out = jnp.concatenate(sums, 0).astype(BF)
    for side in range(sides):
        tap_ref[side * tap_rows : (side + 1) * tap_rows] = out[:, side * 128 : (side + 1) * 128]


def spread_kernel(pieces, members, proj_ref, *rest):
    n_heads = len(rest) - members - 4
    xs, go_refs = rest[:n_heads], rest[n_heads : n_heads + members]
    piece_ref, full, go_buf, piece_buf = rest[n_heads + members :]
    rows, width = xs[0].shape
    half = rows // 2
    mine = lax.axis_index("head")
    for k in range(n_heads):
        full[mine ^ k] = xs[k][...]
    go = jnp.zeros((rows, proj_ref.shape[1]), F32)
    for b in range(n_heads):
        go = go + dot(full[b], proj_ref[b * width : (b + 1) * width], ((1,), (0,)))
    go = go.astype(BF)
    for m in range(members):
        cols = slice(m * HEAD_DIM, (m + 1) * HEAD_DIM)
        go_buf[m, :, 0:HEAD_DIM] = go[0:half, cols]
        go_buf[m, :, HEAD_DIM:] = go[half:, cols]
        for i, first in enumerate(pieces[m]):
            piece_buf[m, i * rows : (i + 1) * rows] = full[first // width][
                :, first % width : first % width + 128
            ]
    me = member(members)
    for k in range(members):
        go_refs[k][...] = go_buf[me ^ k]
        piece_ref[k] = piece_buf[me ^ k]


def widened(x, keep_high):
    x = x.astype(F32)
    turned = pltpu.roll(x, HEAD_DIM, 1)
    lane = lax.broadcasted_iota(jnp.int32, x.shape, 1)
    used = (lane >= HEAD_DIM) if keep_high else (lane < HEAD_DIM)
    first, second = (turned, x) if keep_high else (x, turned)
    return jnp.concatenate([jnp.where(used, first, 0.0), jnp.where(used, second, 0.0)], 0)


def over(count, body):
    if count <= 2:
        for g in range(count):
            body(g)
    else:
        lax.fori_loop(0, count, lambda g, c: (body(g), c)[1], 0)


def key_block(refs, g):
    return refs[0][g] if len(refs) == 1 else refs[g][...]


def queries_of(got_refs, scale):
    rows = got_refs[0].shape[0] * 2 // 3
    q = jnp.concatenate([r[rows:, :] for r in got_refs], 0)
    return (widened(q, False) * scale).astype(BF)


def forward_kernel(n_keys, members, scale, len_ref, piece_ref, tap_ref, *rest):
    got, rest = rest[:members], rest[members:]
    kv, rest = rest[:n_keys], rest[n_keys:]
    p_ref, slots, (s_ref, m_ref, l_ref, acc_ref) = rest[0], rest[1 : 1 + members], rest[1 + members :]
    groups, keys, queries = s_ref.shape
    rows = keys // members
    total = total_of(len_ref)
    ctx = lax.axis_index("ctx")
    me, group = lax.rem(ctx, members), lax.div(ctx, members)
    q = queries_of(got, scale)
    m_ref[...] = jnp.full(m_ref.shape, -1e30, F32)
    l_ref[...] = jnp.zeros(l_ref.shape, F32)
    acc_ref[...] = jnp.zeros(acc_ref.shape, F32)

    def scores(g):
        s = dot(key_block(kv, g), q, ((1,), (1,)))
        start = (lax.rem(group + g, groups) if n_keys > 1 else g) * keys
        s_ref[g] = s

        @pl.when(start + keys > total)
        def _():
            for k in range(members):
                pos = start + (me ^ k) * rows + lax.broadcasted_iota(jnp.int32, (rows, queries), 0)
                part = s_ref[g, k * rows : (k + 1) * rows]
                s_ref[g, k * rows : (k + 1) * rows] = jnp.where(pos < total, part, -1e30)

        m_ref[...] = jnp.maximum(m_ref[...], jnp.max(s_ref[g], axis=0, keepdims=True))

    over(groups, scores)

    def weights(g):
        e = jnp.exp(s_ref[g] - m_ref[...])
        s_ref[g] = e
        l_ref[...] += jnp.sum(e, axis=0, keepdims=True)

    over(groups, weights)
    l_ref[...] = 1.0 / l_ref[...]

    def values(g):
        p = (s_ref[g] * l_ref[...]).astype(BF)
        p_ref[g] = p
        acc_ref[...] += dot(key_block(kv, g), p, ((0,), (0,)))

    over(groups, values)
    attn = acc_ref[HEAD_DIM:, :].T.astype(BF)
    half = queries // 2
    count = piece_ref.shape[1]
    for k in range(members):
        slots[k][0:count] = piece_ref[k]
        slots[k][count : count + half, 0:HEAD_DIM] = attn[0:half]
        slots[k][count : count + half, HEAD_DIM:] = attn[half:]
        slots[k][count + half :] = tap_ref[...]


def backward_kernel(n_keys, members, scale, p_ref, *rest):
    got, rest = rest[:members], rest[members:]
    gos, rest = rest[:members], rest[members:]
    kv, rest = rest[:n_keys], rest[n_keys:]
    dkv, (dq_ref, s_ref, d_ref, acc_ref) = rest[:n_keys], rest[n_keys:]
    groups, _, queries = s_ref.shape
    q = queries_of(got, scale)
    go = widened(jnp.concatenate([r[...] for r in gos], 0), True).astype(BF)
    d_ref[...] = jnp.zeros(d_ref.shape, F32)
    acc_ref[...] = jnp.zeros(acc_ref.shape, F32)

    def slopes(g):
        s = dot(key_block(kv, g), go, ((1,), (1,)))
        s_ref[g] = s
        d_ref[...] += jnp.sum(s * p_ref[g].astype(F32), axis=0, keepdims=True)

    over(groups, slopes)

    def grads(g):
        p = p_ref[g]
        ds = (p.astype(F32) * (s_ref[g] - d_ref[...])).astype(BF)
        acc_ref[...] += dot(key_block(kv, g), ds, ((0,), (0,)))
        out = (dot(ds, q, ((1,), (0,))) + dot(p, go, ((1,), (0,)))).astype(BF)
        if n_keys > 1:
            dkv[g][...] = out
        else:
            dkv[0][g] = out

    over(groups, grads)
    dq = (acc_ref[0:HEAD_DIM, :] * scale).T.astype(BF)
    half = queries // 2
    dq_ref[:, 0:HEAD_DIM] = dq[0:half]
    dq_ref[:, HEAD_DIM:] = dq[half:]


def project_kernel(own_rows, members, *refs):
    slots, outs, (lhs, rhs, heads) = refs[:members], refs[members:-3], refs[-3:]
    out_ref, tap_ref = outs[:2]
    count, width = lhs.shape[1], rhs.shape[1]
    half = lhs.shape[0] // members
    rows = 2 * half
    me = member(members)
    first = count // 128 * rows
    acc = jnp.zeros((count, width), F32)
    tap = jnp.zeros((slots[0].shape[0] - first - members * half, 128), F32)
    for k in range(members):
        heads[me ^ k] = slots[k][first : first + members * half]
        tap = tap + slots[k][first + members * half :].astype(F32)
    tap_ref[...] = tap.astype(BF)
    for fold in range(2):
        for k in range(members):
            for side in range(count // 128):
                at = side * rows + fold * half
                where = pl.multiple_of((me ^ k) * half, half)
                lhs[pl.ds(where, half), side * 128 : (side + 1) * 128] = slots[k][at : at + half]
        for h in range(members):
            for i in range(members):
                j = h ^ i
                rhs[i * half : (i + 1) * half, h * HEAD_DIM : (h + 1) * HEAD_DIM] = heads[
                    h, j * half : (j + 1) * half, fold * HEAD_DIM : (fold + 1) * HEAD_DIM
                ]
        acc = acc + dot(lhs[...], rhs[...], ((0,), (0,)))
    if len(outs) == 2:
        out_ref[...] = acc
        return
    send_ref = outs[2]
    first = lax.axis_index("ctx") < lax.axis_size("ctx") // 2
    low, high = acc[:own_rows], acc[own_rows:]
    out_ref[...] = jnp.where(first, low, high)
    theirs = jnp.where(first, high, low).astype(BF)
    for side in range(width // 128):
        send_ref[side * own_rows : (side + 1) * own_rows] = theirs[:, side * 128 : (side + 1) * 128]
    send_ref[width // 128 * own_rows :] = tap.astype(BF)


def collect_kernel(members, *refs):
    parts, dq_ref, slots = refs[: -1 - members], refs[-1 - members], refs[-members:]
    rows = slots[0].shape[0] * 2 // 3
    half = rows // 2
    if len(parts) == 1:
        total = parts[0][0].astype(F32)
        for g in range(1, parts[0].shape[0]):
            total = total + parts[0][g].astype(F32)
    else:
        total = parts[0][...].astype(F32) + parts[1][...].astype(F32)
    total = total.astype(BF)
    for k in range(members):
        slots[k][0:rows] = total[k * rows : (k + 1) * rows]
        slots[k][rows:] = dq_ref[k * half : (k + 1) * half]


def unpack_kernel(*refs):
    members = len(refs) - 4
    slots, (q_ref, k_ref, v_ref, buf) = refs[:members], refs[members:]
    rows = q_ref.shape[0]
    half = rows // 2
    me = member(members)
    for k in range(members):
        buf[me ^ k] = slots[k][...]
    for m in range(members):
        cols = slice(m * HEAD_DIM, (m + 1) * HEAD_DIM)
        k_ref[:, cols] = buf[m, 0:rows, 0:HEAD_DIM]
        v_ref[:, cols] = buf[m, 0:rows, HEAD_DIM:]
        q_ref[0:half, cols] = buf[m, rows:, 0:HEAD_DIM]
        q_ref[half:, cols] = buf[m, rows:, HEAD_DIM:]


def finish_kernel(mine_ref, tap_ref, got_ref, out_ref, grad_ref):
    own_rows, width = mine_ref.shape
    taps = grad_ref.shape[0]
    sides = width // 128
    tap_rows = tap_ref.shape[0] // sides
    tap = tap_ref[...].astype(F32) + got_ref[sides * own_rows :].astype(F32)
    for side in range(sides):
        cols = slice(side * 128, (side + 1) * 128)
        out_ref[:, cols] = mine_ref[:, cols] + got_ref[
            side * own_rows : (side + 1) * own_rows
        ].astype(F32)
        grad_ref[:, cols] = tap[side * tap_rows : side * tap_rows + taps]


def on_device(
    query_all, key_all, value_all, cotangent, conv_input, rec_lengths, out_proj, conv_weight
):
    rows, width = query_all.shape
    half = rows // 2
    members = width // HEAD_DIM
    n_ctx, n_heads = lax.axis_size("ctx"), lax.axis_size("head")
    groups = n_ctx // members
    channels = out_proj.shape[0]
    own_rows = channels // n_ctx
    scale = HEAD_DIM**-0.5
    taps = conv_weight.shape[0]
    tap_rows = -(-taps // 16) * 16
    sides = width // 128
    keys = members * rows
    queries = members * rows
    pair = groups == 2
    across = [[g * members + m for g in range(groups)] for m in range(members)]
    other = [(i, (i + members) % n_ctx) for i in range(n_ctx)]

    def swap(slots, axis="ctx"):
        n = lax.axis_size(axis)
        return [slots[0]] + [
            move(slots[k], [(i, i ^ k) for i in range(n)], axis) for k in range(1, len(slots))
        ]

    def move(x, pairs, axis="ctx"):
        return lax.ppermute(x, axis, pairs)

    up, down = call(
        halo_kernel, (shape((HALO_X + HALO_G, width), BF),) * 2, (conv_input, cotangent)
    )
    low = move(up, [(i, i + 1) for i in range(n_ctx - 1)])
    high = move(down, [(i + 1, i) for i in range(n_ctx - 1)])
    slot = shape((rows + half, 128), BF)
    got = swap(
        call(
            pack_kernel,
            (slot,) * members,
            (query_all, key_all, value_all, up),
            scratch=[pltpu.VMEM((members, rows + half, 128), BF)],
        ),
    )
    x_grad, x_send, grad_conv = call(
        conv_kernel,
        (shape((rows, width), BF),) * 3,
        (rec_lengths, conv_input, cotangent, low, high, conv_weight),
        smem=1,
        scratch=[
            pltpu.VMEM((rows + 2 * HALO_X, width), F32),
            pltpu.VMEM((rows + 2 * HALO_G, width), F32),
        ],
    )
    xs = swap([x_send] * n_heads, "head")
    own_kv = call(join_kernel, shape((keys, 128), BF), (grad_conv, *got))
    if pair:
        kv = (own_kv, move(own_kv, other))
    else:
        kv = (lax.all_gather(own_kv, "ctx", axis_index_groups=across),)
    n_keys = len(kv)
    tap_part = call(
        functools.partial(taps_kernel, taps),
        shape((sides * tap_rows, 128), BF),
        (rec_lengths, conv_input, low, high, grad_conv),
        smem=1,
        scratch=[pltpu.VMEM((rows + 2 * HALO_X, width), F32)],
    )
    count = groups * own_rows
    if own_rows % 128 == 0:
        pieces = [
            [(g * members + m) * own_rows + b for g in range(groups) for b in range(0, own_rows, 128)]
            for m in range(members)
        ]
    else:
        pieces = [list(range(m * count, (m + 1) * count, 128)) for m in range(members)]
    spread = call(
        functools.partial(spread_kernel, pieces, members),
        (shape((half, 128), BF),) * members + (shape((members, count // 128 * rows, 128), BF),),
        (out_proj, *xs),
        scratch=[
            pltpu.VMEM((n_heads, rows, width), BF),
            pltpu.VMEM((members, half, 128), BF),
            pltpu.VMEM((members, count // 128 * rows, 128), BF),
        ],
        flops=2 * rows * channels * width,
    )
    piece = spread[members]
    gos = swap(spread[:members])
    big = (12 << 20) if groups <= 2 else (60 << 20)
    flops = 2 * queries * keys * groups * 128
    fwd = call(
        functools.partial(forward_kernel, n_keys, members, scale),
        (shape((groups, keys, queries), BF),)
        + (shape((count // 128 * rows + queries // 2 + sides * tap_rows, 128), BF),) * members,
        (rec_lengths, piece, tap_part, *got, *kv),
        smem=1,
        scratch=[
            pltpu.VMEM((groups, keys, queries), F32),
            pltpu.VMEM((1, queries), F32),
            pltpu.VMEM((1, queries), F32),
            pltpu.VMEM((128, queries), F32),
        ],
        flops=2 * flops,
        limit=big,
    )
    probs = fwd[0]
    bwd = call(
        functools.partial(backward_kernel, n_keys, members, scale),
        (
            (shape((keys, 128), BF),) * 2
            if pair
            else (shape((groups, keys, 128), BF),)
        )
        + (shape((queries // 2, 128), BF),),
        (probs, *got, *gos, *kv),
        scratch=[
            pltpu.VMEM((groups, keys, queries), F32),
            pltpu.VMEM((1, queries), F32),
            pltpu.VMEM((128, queries), F32),
        ],
        flops=4 * flops,
        limit=big,
    )
    dq = bwd[-1]
    if pair:
        parts = (bwd[0], move(bwd[1], other))
    else:
        parts = (lax.all_to_all(bwd[0], "ctx", 0, 0, axis_index_groups=across),)
    back = swap(call(functools.partial(collect_kernel, members), (slot,) * members, (*parts, dq)))
    q_grad, k_grad, v_grad = call(
        unpack_kernel,
        (shape((rows, width), BF),) * 3,
        tuple(back),
        scratch=[pltpu.VMEM((members, rows + half, 128), BF)],
    )
    shared = swap(fwd[1:])
    merged = pair and own_rows % 16 == 0
    tap_shape = shape((sides * tap_rows, 128), BF)
    outs = (
        (shape((own_rows, width), F32), tap_shape, shape((sides * (own_rows + tap_rows), 128), BF))
        if merged
        else (shape((count, width), F32), tap_shape)
    )
    partial, tap_sum, *send = call(
        functools.partial(project_kernel, own_rows, members),
        outs,
        tuple(shared),
        scratch=[
            pltpu.VMEM((members * half, count), BF),
            pltpu.VMEM((members * half, width), BF),
            pltpu.VMEM((members, queries // 2, 128), BF),
        ],
        flops=2 * count * width * queries,
    )
    grads = (shape((own_rows, width), F32), shape((taps, width), F32))
    if merged:
        out_proj_grad, conv_weight_grad = call(
            finish_kernel, grads, (partial, tap_sum, move(send[0], other))
        )
    else:
        if own_rows % 128:
            wanted = partial.astype(BF).reshape(1, groups, own_rows, width)
            slots = jnp.zeros((members, groups, own_rows, width), BF)
            slots = lax.dynamic_update_slice(
                slots, wanted, (lax.rem(lax.axis_index("ctx"), members), 0, 0, 0)
            )
            moved = lax.all_to_all(slots.reshape(n_ctx, own_rows, width), "ctx", 0, 0)
        else:
            moved = lax.all_to_all(
                partial.astype(BF).reshape(groups, own_rows, width),
                "ctx",
                0,
                0,
                axis_index_groups=across,
            )
        out_proj_grad = jnp.sum(moved.astype(F32), 0)
        tap_all = jnp.sum(
            lax.all_gather(tap_sum, "ctx", axis_index_groups=across).astype(F32), 0
        ).reshape(sides, tap_rows, 128)
        conv_weight_grad = jnp.swapaxes(tap_all, 0, 1).reshape(tap_rows, width)[:taps]
    return (q_grad, k_grad, v_grad, x_grad, out_proj_grad, conv_weight_grad)


def solution(mesh):
    placed = (
        P("ctx", "head"),
        P("ctx", "head"),
        P("ctx", "head"),
        P("ctx", "head"),
        P("ctx", "head"),
        P(),
        P(None, "head"),
        P(None, "head"),
    )

    return jax.shard_map(
        on_device,
        mesh=mesh,
        in_specs=placed,
        out_specs=(
            P("ctx", "head"),
            P("ctx", "head"),
            P("ctx", "head"),
            P("ctx", "head"),
            P("ctx", "head"),
            P(None, "head"),
        ),
        check_vma=False,
    )
```

```python
import functools

import jax
import jax.numpy as jnp
from jax import lax
from jax.experimental import pallas as pl
from jax.experimental.pallas import tpu as pltpu
from jax.sharding import PartitionSpec as P


HEAD_DIM = 64
HALO_X = 32
HALO_G = 16
BF = jnp.bfloat16
F32 = jnp.float32
VM = pl.BlockSpec(memory_space=pltpu.VMEM)
HB = pl.BlockSpec(memory_space=pltpu.HBM)
SM = pl.BlockSpec(memory_space=pltpu.SMEM)


def dot(a, b, dims):
    return lax.dot_general(a, b, (dims, ((), ())), preferred_element_type=F32)


def call(kernel, out_shape, args, smem=0, hbm=0, scratch=(), flops=1 << 20, limit=None):
    one = not isinstance(out_shape, (tuple, list))
    return pl.pallas_call(
        kernel,
        out_shape=out_shape,
        in_specs=[SM] * smem + [HB] * hbm + [VM] * (len(args) - smem - hbm),
        out_specs=VM if one else tuple(VM for _ in out_shape),
        scratch_shapes=list(scratch),
        compiler_params=pltpu.CompilerParams(vmem_limit_bytes=limit or (4 << 20)),
        cost_estimate=pl.CostEstimate(flops=flops, bytes_accessed=1 << 20, transcendentals=0),
    )(*args)


def shape(dims, dtype):
    return jax.ShapeDtypeStruct(tuple(dims), dtype)


OUTER = False


def ctx_of(m, g, members, groups):
    return m * groups + g if OUTER else g * members + m


def member(members, ctx=None):
    ctx = lax.axis_index("ctx") if ctx is None else ctx
    return ctx // (lax.axis_size("ctx") // members) if OUTER else ctx % members


def group_of(members, ctx=None):
    ctx = lax.axis_index("ctx") if ctx is None else ctx
    return ctx % (lax.axis_size("ctx") // members) if OUTER else ctx // members


def total_of(lengths_ref):
    total = lengths_ref[0]
    for i in range(1, lengths_ref.shape[0]):
        total = total + lengths_ref[i]
    return total


def start_kernel(members, *refs):
    q_hbm, k_hbm, v_hbm, x_hbm, g_hbm, w_hbm, x_ref, g_ref, w_ref, up_ref, down_ref, *rest = refs
    slots, (q_ref, k_ref, v_ref, buf, sems) = rest[:members], rest[members:]
    rows = q_ref.shape[0]
    half = rows // 2
    moves = (
        (x_hbm, x_ref),
        (g_hbm, g_ref),
        (k_hbm, k_ref),
        (v_hbm, v_ref),
        (q_hbm, q_ref),
        (w_hbm, w_ref),
    )
    copies = [pltpu.make_async_copy(a, b, sems.at[i]) for i, (a, b) in enumerate(moves)]
    for copy in copies:
        copy.start()
    for copy in copies:
        copy.wait()
    up_ref[0:HALO_X] = x_ref[rows - HALO_X :]
    up_ref[HALO_X:] = g_ref[rows - HALO_G :]
    down_ref[0:HALO_X] = x_ref[0:HALO_X]
    down_ref[HALO_X:] = g_ref[0:HALO_G]
    for m in range(members):
        cols = slice(m * HEAD_DIM, (m + 1) * HEAD_DIM)
        buf[m, 0:rows, 0:HEAD_DIM] = k_ref[:, cols]
        buf[m, 0:rows, HEAD_DIM:] = v_ref[:, cols]
        buf[m, rows:, 0:HEAD_DIM] = q_ref[0:half, cols]
        buf[m, rows:, HEAD_DIM:] = q_ref[half:, cols]
    me = member(members)
    for k in range(members):
        slots[k][...] = buf[me ^ k]


def join_kernel(after_ref, *refs):
    out_ref = refs[-1]
    rows = out_ref.shape[0] // (len(refs) - 1)
    for k, ref in enumerate(refs[:-1]):
        out_ref[k * rows : (k + 1) * rows] = ref[0:rows]


def masked_into(xs, len_ref, x_ref, low_ref, high_ref):
    rows = x_ref.shape[0]
    base = lax.axis_index("ctx") * rows - HALO_X
    total = total_of(len_ref)
    for c in range(xs.shape[0]):
        cols = slice(c * 128, (c + 1) * 128)
        xs[c, 0:HALO_X] = low_ref[0:HALO_X, cols].astype(F32)
        xs[c, HALO_X : HALO_X + rows] = x_ref[:, cols].astype(F32)
        xs[c, HALO_X + rows :] = high_ref[0:HALO_X, cols].astype(F32)

    @pl.when(base + xs.shape[1] > total)
    def _():
        for c in range(xs.shape[0]):
            pos = base + lax.broadcasted_iota(jnp.int32, xs.shape[1:], 0)
            xs[c] = jnp.where(pos < total, xs[c], 0.0)


def conv_kernel(
    len_ref, x_ref, g_ref, low_ref, high_ref, w_ref, out_ref, send_ref, mine_ref, xs, gs
):
    rows = x_ref.shape[0]
    taps = w_ref.shape[0]
    half = taps // 2
    wide = rows + 2 * HALO_G
    shift = HALO_X - HALO_G - half
    total = total_of(len_ref)
    masked_into(xs, len_ref, x_ref, low_ref, high_ref)
    for c in range(xs.shape[0]):
        cols = slice(c * 128, (c + 1) * 128)
        w = w_ref[:, cols].astype(F32)
        acc = jnp.zeros((wide, 128), F32)
        for j in range(taps):
            acc = acc + w[j : j + 1] * xs[c, shift + j : shift + j + wide]
        s = jax.nn.sigmoid(acc)
        slope = s * (1.0 + acc * (1.0 - s))
        gs[c, 0:HALO_G] = low_ref[HALO_X:, cols].astype(F32)
        gs[c, HALO_G : HALO_G + rows] = g_ref[:, cols].astype(F32)
        gs[c, HALO_G + rows :] = high_ref[HALO_X:, cols].astype(F32)
        gs[c] = (gs[c] * slope).astype(BF).astype(F32)
        acc = jnp.zeros((rows, 128), F32)
        for j in range(taps):
            first = HALO_G + half - j
            acc = acc + w[j : j + 1] * gs[c, first : first + rows]
        pos = lax.axis_index("ctx") * rows + lax.broadcasted_iota(jnp.int32, acc.shape, 0)
        acc = jnp.where(pos < total, acc, 0.0)
        out = (g_ref[:, cols].astype(F32) + acc).astype(BF)
        out_ref[:, cols] = out
        send_ref[:, cols] = out
        mine_ref[:, cols] = gs[c, HALO_G : HALO_G + rows].astype(BF)


def taps_kernel(taps, len_ref, x_ref, low_ref, high_ref, mine_ref, after_ref, tap_ref, xs):
    rows = x_ref.shape[0]
    half = taps // 2
    sides = xs.shape[0]
    tap_rows = tap_ref.shape[0] // sides
    masked_into(xs, len_ref, x_ref, low_ref, high_ref)
    for c in range(sides):
        mine = mine_ref[:, c * 128 : (c + 1) * 128].astype(F32)
        sums = []
        for j in range(taps):
            first = HALO_X - half + j
            sums.append(jnp.sum(mine * xs[c, first : first + rows], axis=0, keepdims=True))
        sums.append(jnp.zeros((tap_rows - taps, 128), F32))
        tap_ref[c * tap_rows : (c + 1) * tap_rows] = jnp.concatenate(sums, 0).astype(BF)


def spread_kernel(pieces, members, proj_ref, *rest):
    n_heads = len(rest) - members - 2
    xs, slots, (full, buf) = rest[:n_heads], rest[n_heads:-2], rest[-2:]
    rows, width = xs[0].shape
    half = rows // 2
    mine = lax.axis_index("head")
    for k in range(n_heads):
        full[mine ^ k] = xs[k][...]
    go = jnp.zeros((rows, proj_ref.shape[1]), F32)
    for b in range(n_heads):
        go = go + dot(full[b], proj_ref[b * width : (b + 1) * width], ((1,), (0,)))
    go = go.astype(BF)
    for m in range(members):
        cols = slice(m * HEAD_DIM, (m + 1) * HEAD_DIM)
        buf[m, 0:half, 0:HEAD_DIM] = go[0:half, cols]
        buf[m, 0:half, HEAD_DIM:] = go[half:, cols]
        for i, first in enumerate(pieces[m]):
            buf[m, half + i * rows : half + (i + 1) * rows] = full[first // width][
                :, first % width : first % width + 128
            ]
    me = member(members)
    for k in range(members):
        slots[k][...] = buf[me ^ k]


def widened(x, keep_high):
    x = x.astype(F32)
    turned = pltpu.roll(x, HEAD_DIM, 1)
    lane = lax.broadcasted_iota(jnp.int32, x.shape, 1)
    used = (lane >= HEAD_DIM) if keep_high else (lane < HEAD_DIM)
    first, second = (turned, x) if keep_high else (x, turned)
    return jnp.concatenate([jnp.where(used, first, 0.0), jnp.where(used, second, 0.0)], 0)


def over(count, body):
    if count <= 2:
        for g in range(count):
            body(g)
    else:
        lax.fori_loop(0, count, lambda g, c: (body(g), c)[1], 0)


def key_block(refs, g):
    return refs[0][g] if len(refs) == 1 else refs[g][...]


def queries_of(got_refs, scale):
    rows = got_refs[0].shape[0] * 2 // 3
    q = jnp.concatenate([r[rows:, :] for r in got_refs], 0)
    return (widened(q, False) * scale).astype(BF)


def forward_kernel(n_keys, members, scale, len_ref, tap_ref, *rest):
    got, rest = rest[:members], rest[members:]
    kv, rest = rest[:n_keys], rest[n_keys:]
    p_ref, slot_ref, s_ref, m_ref, l_ref, acc_ref = rest
    groups, keys, queries = s_ref.shape
    rows = keys // members
    total = total_of(len_ref)
    me, group = member(members), group_of(members)
    q = queries_of(got, scale)
    m_ref[...] = jnp.full(m_ref.shape, -1e30, F32)
    l_ref[...] = jnp.zeros(l_ref.shape, F32)
    acc_ref[...] = jnp.zeros(acc_ref.shape, F32)

    def scores(g):
        s = dot(key_block(kv, g), q, ((1,), (1,)))
        from_group = lax.rem(group + g, groups) if n_keys > 1 else g
        s_ref[g] = s

        @pl.when((ctx_of(members - 1, from_group, members, groups) + 1) * rows > total)
        def _():
            for k in range(members):
                start = ctx_of(me ^ k, from_group, members, groups) * rows
                pos = start + lax.broadcasted_iota(jnp.int32, (rows, queries), 0)
                part = s_ref[g, k * rows : (k + 1) * rows]
                s_ref[g, k * rows : (k + 1) * rows] = jnp.where(pos < total, part, -1e30)

        m_ref[...] = jnp.maximum(m_ref[...], jnp.max(s_ref[g], axis=0, keepdims=True))

    over(groups, scores)

    def weights(g):
        e = jnp.exp(s_ref[g] - m_ref[...])
        s_ref[g] = e
        l_ref[...] += jnp.sum(e, axis=0, keepdims=True)

    over(groups, weights)
    l_ref[...] = 1.0 / l_ref[...]

    def values(g):
        p = (s_ref[g] * l_ref[...]).astype(BF)
        p_ref[g] = p
        acc_ref[...] += dot(key_block(kv, g), p, ((0,), (0,)))

    over(groups, values)
    attn = acc_ref[HEAD_DIM:, :].T.astype(BF)
    half = queries // 2
    slot_ref[0:half, 0:HEAD_DIM] = attn[0:half]
    slot_ref[0:half, HEAD_DIM:] = attn[half:]
    slot_ref[half:] = tap_ref[...]


def backward_kernel(n_keys, members, scale, p_ref, *rest):
    got, rest = rest[:members], rest[members:]
    gos, rest = rest[:members], rest[members:]
    kv, rest = rest[:n_keys], rest[n_keys:]
    dkv, (dq_ref, s_ref, d_ref, acc_ref) = rest[:n_keys], rest[n_keys:]
    groups, _, queries = s_ref.shape
    q = queries_of(got, scale)
    half = queries // members // 2
    go = widened(jnp.concatenate([r[0:half] for r in gos], 0), True).astype(BF)
    d_ref[...] = jnp.zeros(d_ref.shape, F32)
    acc_ref[...] = jnp.zeros(acc_ref.shape, F32)

    def slopes(g):
        s = dot(key_block(kv, g), go, ((1,), (1,)))
        s_ref[g] = s
        d_ref[...] += jnp.sum(s * p_ref[g].astype(F32), axis=0, keepdims=True)

    over(groups, slopes)

    def grads(g):
        p = p_ref[g]
        ds = (p.astype(F32) * (s_ref[g] - d_ref[...])).astype(BF)
        acc_ref[...] += dot(key_block(kv, g), ds, ((0,), (0,)))
        out = (dot(ds, q, ((1,), (0,))) + dot(p, go, ((1,), (0,)))).astype(BF)
        if n_keys > 1:
            dkv[g][...] = out
        else:
            dkv[0][g] = out

    over(groups, grads)
    dq = (acc_ref[0:HEAD_DIM, :] * scale).T.astype(BF)
    half = queries // 2
    dq_ref[:, 0:HEAD_DIM] = dq[0:half]
    dq_ref[:, HEAD_DIM:] = dq[half:]


def project_kernel(own_rows, members, *refs):
    gos, slots = refs[:members], refs[members : 2 * members]
    outs, (lhs, rhs, heads) = refs[2 * members : -3], refs[-3:]
    out_ref, tap_ref = outs[:2]
    count, width = lhs.shape[1], rhs.shape[1]
    half = lhs.shape[0] // members
    rows = 2 * half
    me = member(members)
    acc = jnp.zeros((count, width), F32)
    tap = jnp.zeros(tap_ref.shape, F32)
    for k in range(members):
        heads[me ^ k] = slots[k][0 : members * half]
        tap = tap + slots[k][members * half :].astype(F32)
    tap_ref[...] = tap.astype(BF)
    for fold in range(2):
        for k in range(members):
            for side in range(count // 128):
                at = half + side * rows + fold * half
                where = pl.multiple_of((me ^ k) * half, half)
                lhs[pl.ds(where, half), side * 128 : (side + 1) * 128] = gos[k][at : at + half]
        for h in range(members):
            for i in range(members):
                j = h ^ i
                rhs[i * half : (i + 1) * half, h * HEAD_DIM : (h + 1) * HEAD_DIM] = heads[
                    h, j * half : (j + 1) * half, fold * HEAD_DIM : (fold + 1) * HEAD_DIM
                ]
        acc = acc + dot(lhs[...], rhs[...], ((0,), (0,)))
    if len(outs) == 2:
        out_ref[...] = acc
        return
    send_ref = outs[2]
    first = group_of(members) == 0
    low, high = acc[:own_rows], acc[own_rows:]
    out_ref[...] = jnp.where(first, low, high)
    theirs = jnp.where(first, high, low).astype(BF)
    for side in range(width // 128):
        send_ref[side * own_rows : (side + 1) * own_rows] = theirs[:, side * 128 : (side + 1) * 128]
    send_ref[width // 128 * own_rows :] = tap.astype(BF)


def collect_kernel(members, *refs):
    parts, dq_ref, slots = refs[: -1 - members], refs[-1 - members], refs[-members:]
    rows = slots[0].shape[0] * 2 // 3
    half = rows // 2
    if len(parts) == 1:
        total = parts[0][0].astype(F32)
        for g in range(1, parts[0].shape[0]):
            total = total + parts[0][g].astype(F32)
    else:
        total = parts[0][...].astype(F32) + parts[1][...].astype(F32)
    total = total.astype(BF)
    for k in range(members):
        slots[k][0:rows] = total[k * rows : (k + 1) * rows]
        slots[k][rows:] = dq_ref[k * half : (k + 1) * half]


def end_kernel(members, *refs):
    finish_kernel(*refs[members : members + 3], *refs[members + 6 : members + 8])
    unpack_kernel(*refs[:members], *refs[members + 3 : members + 6], refs[-1])


def unpack_kernel(*refs):
    members = len(refs) - 4
    slots, (q_ref, k_ref, v_ref, buf) = refs[:members], refs[members:]
    rows = q_ref.shape[0]
    half = rows // 2
    me = member(members)
    for k in range(members):
        buf[me ^ k] = slots[k][...]
    for m in range(members):
        cols = slice(m * HEAD_DIM, (m + 1) * HEAD_DIM)
        k_ref[:, cols] = buf[m, 0:rows, 0:HEAD_DIM]
        v_ref[:, cols] = buf[m, 0:rows, HEAD_DIM:]
        q_ref[0:half, cols] = buf[m, rows:, 0:HEAD_DIM]
        q_ref[half:, cols] = buf[m, rows:, HEAD_DIM:]


def finish_kernel(mine_ref, tap_ref, got_ref, out_ref, grad_ref):
    own_rows, width = mine_ref.shape
    taps = grad_ref.shape[0]
    sides = width // 128
    tap_rows = tap_ref.shape[0] // sides
    tap = tap_ref[...].astype(F32) + got_ref[sides * own_rows :].astype(F32)
    for side in range(sides):
        cols = slice(side * 128, (side + 1) * 128)
        out_ref[:, cols] = mine_ref[:, cols] + got_ref[
            side * own_rows : (side + 1) * own_rows
        ].astype(F32)
        grad_ref[:, cols] = tap[side * tap_rows : side * tap_rows + taps]


def on_device(
    query_all, key_all, value_all, cotangent, conv_input, rec_lengths, out_proj, conv_weight
):
    rows, width = query_all.shape
    half = rows // 2
    members = width // HEAD_DIM
    n_ctx, n_heads = lax.axis_size("ctx"), lax.axis_size("head")
    groups = n_ctx // members
    channels = out_proj.shape[0]
    own_rows = channels // n_ctx
    scale = HEAD_DIM**-0.5
    taps = conv_weight.shape[0]
    tap_rows = -(-taps // 16) * 16
    sides = width // 128
    keys = members * rows
    queries = members * rows
    pair = groups == 2
    across = [[ctx_of(m, g, members, groups) for g in range(groups)] for m in range(members)]

    def partners(change):
        return [
            (i, ctx_of(*change(member(members, i), group_of(members, i)), members, groups))
            for i in range(n_ctx)
        ]

    other = partners(lambda m, g: (m, (g + 1) % groups))

    def swap(slots, axis="ctx"):
        def by_xor(k):
            if axis == "ctx":
                return partners(lambda m, g: (m ^ k, g))
            return [(i, i ^ k) for i in range(n_heads)]

        return [slots[0]] + [move(slots[k], by_xor(k), axis) for k in range(1, len(slots))]

    def move(x, pairs, axis="ctx"):
        return lax.ppermute(x, axis, pairs)

    slot = shape((rows + half, 128), BF)
    halo = shape((HALO_X + HALO_G, width), BF)
    given = (query_all, key_all, value_all, conv_input, cotangent, conv_weight)
    x_in, g_in, w_in, up, down, *slots = call(
        functools.partial(start_kernel, members),
        (shape((rows, width), BF),) * 2
        + (shape(conv_weight.shape, BF), halo, halo)
        + (slot,) * members,
        tuple(pltpu.with_memory_space_constraint(x, pltpu.HBM) for x in given),
        hbm=len(given),
        scratch=[pltpu.VMEM((rows, width), BF)] * 3
        + [pltpu.VMEM((members, rows + half, 128), BF), pltpu.SemaphoreType.DMA((len(given),))],
    )
    low = move(up, [(i, i + 1) for i in range(n_ctx - 1)])
    high = move(down, [(i + 1, i) for i in range(n_ctx - 1)])
    got = swap(slots)
    x_grad, x_send, grad_conv = call(
        conv_kernel,
        (shape((rows, width), BF),) * 3,
        (rec_lengths, x_in, g_in, low, high, w_in),
        smem=1,
        scratch=[
            pltpu.VMEM((sides, rows + 2 * HALO_X, 128), F32),
            pltpu.VMEM((sides, rows + 2 * HALO_G, 128), F32),
        ],
    )
    xs = swap([x_send] * n_heads, "head")
    own_kv = call(join_kernel, shape((keys, 128), BF), (grad_conv, *got))
    if pair:
        kv = (own_kv, move(own_kv, other))
    else:
        kv = (lax.all_gather(own_kv, "ctx", axis_index_groups=across),)
    n_keys = len(kv)
    count = groups * own_rows
    aligned = OUTER or own_rows % 128 == 0
    pieces = [
        [ctx_of(m, g, members, groups) * own_rows + b for g in range(groups) for b in range(0, own_rows, 128)]
        if own_rows % 128 == 0
        else list(range(m * count, (m + 1) * count, 128))
        for m in range(members)
    ]
    gradient_rows = half + count // 128 * rows
    spread = call(
        functools.partial(spread_kernel, pieces, members),
        (shape((gradient_rows, 128), BF),) * members,
        (out_proj, *xs),
        scratch=[
            pltpu.VMEM((n_heads, rows, width), BF),
            pltpu.VMEM((members, gradient_rows, 128), BF),
        ],
        flops=2 * rows * channels * width,
    )
    gos = swap(spread)
    tap_part = call(
        functools.partial(taps_kernel, taps),
        shape((sides * tap_rows, 128), BF),
        (rec_lengths, x_in, low, high, grad_conv, spread[0]),
        smem=1,
        scratch=[pltpu.VMEM((sides, rows + 2 * HALO_X, 128), F32)],
    )
    big = (12 << 20) if groups <= 2 else (60 << 20)
    flops = 2 * queries * keys * groups * 128
    fwd = call(
        functools.partial(forward_kernel, n_keys, members, scale),
        (
            shape((groups, keys, queries), BF),
            shape((queries // 2 + sides * tap_rows, 128), BF),
        ),
        (rec_lengths, tap_part, *got, *kv),
        smem=1,
        scratch=[
            pltpu.VMEM((groups, keys, queries), F32),
            pltpu.VMEM((1, queries), F32),
            pltpu.VMEM((1, queries), F32),
            pltpu.VMEM((128, queries), F32),
        ],
        flops=2 * flops,
        limit=big,
    )
    probs = fwd[0]
    bwd = call(
        functools.partial(backward_kernel, n_keys, members, scale),
        (
            (shape((keys, 128), BF),) * 2
            if pair
            else (shape((groups, keys, 128), BF),)
        )
        + (shape((queries // 2, 128), BF),),
        (probs, *got, *gos, *kv),
        scratch=[
            pltpu.VMEM((groups, keys, queries), F32),
            pltpu.VMEM((1, queries), F32),
            pltpu.VMEM((128, queries), F32),
        ],
        flops=4 * flops,
        limit=big,
    )
    dq = bwd[-1]
    if pair:
        parts = (bwd[0], move(bwd[1], other))
    else:
        parts = (lax.all_to_all(bwd[0], "ctx", 0, 0, axis_index_groups=across),)
    back = swap(call(functools.partial(collect_kernel, members), (slot,) * members, (*parts, dq)))
    shared = swap([fwd[1]] * members)
    merged = pair and own_rows % 16 == 0
    tap_shape = shape((sides * tap_rows, 128), BF)
    outs = (
        (shape((own_rows, width), F32), tap_shape, shape((sides * (own_rows + tap_rows), 128), BF))
        if merged
        else (shape((count, width), F32), tap_shape)
    )
    partial, tap_sum, *send = call(
        functools.partial(project_kernel, own_rows, members),
        outs,
        (*gos, *shared),
        scratch=[
            pltpu.VMEM((members * half, count), BF),
            pltpu.VMEM((members * half, width), BF),
            pltpu.VMEM((members, queries // 2, 128), BF),
        ],
        flops=2 * count * width * queries,
    )
    grads = (shape((rows, width), BF),) * 3
    buf = [pltpu.VMEM((members, rows + half, 128), BF)]
    if merged:
        q_grad, k_grad, v_grad, out_proj_grad, conv_weight_grad = call(
            functools.partial(end_kernel, members),
            grads + (shape((own_rows, width), F32), shape((taps, width), F32)),
            (*back, partial, tap_sum, move(send[0], other)),
            scratch=buf,
        )
    else:
        q_grad, k_grad, v_grad = call(unpack_kernel, grads, tuple(back), scratch=buf)
        if not aligned:
            wanted = partial.astype(BF).reshape(1, groups, own_rows, width)
            slots = jnp.zeros((members, groups, own_rows, width), BF)
            slots = lax.dynamic_update_slice(
                slots, wanted, (member(members), 0, 0, 0)
            )
            moved = lax.all_to_all(slots.reshape(n_ctx, own_rows, width), "ctx", 0, 0)
        else:
            moved = lax.all_to_all(
                partial.astype(BF).reshape(groups, own_rows, width),
                "ctx",
                0,
                0,
                axis_index_groups=across,
            )
        out_proj_grad = jnp.sum(moved.astype(F32), 0)
        tap_all = jnp.sum(
            lax.all_gather(tap_sum, "ctx", axis_index_groups=across).astype(F32), 0
        ).reshape(sides, tap_rows, 128)
        conv_weight_grad = jnp.swapaxes(tap_all, 0, 1).reshape(tap_rows, width)[:taps]
    return (q_grad, k_grad, v_grad, x_grad, out_proj_grad, conv_weight_grad)


def solution(mesh):
    placed = (
        P("ctx", "head"),
        P("ctx", "head"),
        P("ctx", "head"),
        P("ctx", "head"),
        P("ctx", "head"),
        P(),
        P(None, "head"),
        P(None, "head"),
    )

    return jax.shard_map(
        on_device,
        mesh=mesh,
        in_specs=placed,
        out_specs=(
            P("ctx", "head"),
            P("ctx", "head"),
            P("ctx", "head"),
            P("ctx", "head"),
            P("ctx", "head"),
            P(None, "head"),
        ),
        check_vma=False,
    )
```

```python
import functools

import jax
import jax.numpy as jnp
from jax import lax
from jax.experimental import pallas as pl
from jax.experimental.pallas import tpu as pltpu
from jax.sharding import PartitionSpec as P


HEAD_DIM = 64
HALO_X = 32
HALO_G = 16
BF = jnp.bfloat16
F32 = jnp.float32
VM = pl.BlockSpec(memory_space=pltpu.VMEM)
HB = pl.BlockSpec(memory_space=pltpu.HBM)
SM = pl.BlockSpec(memory_space=pltpu.SMEM)


def dot(a, b, dims):
    return lax.dot_general(a, b, (dims, ((), ())), preferred_element_type=F32)


def call(kernel, out_shape, args, smem=0, hbm=0, scratch=(), flops=1 << 20, limit=None):
    one = not isinstance(out_shape, (tuple, list))
    return pl.pallas_call(
        kernel,
        out_shape=out_shape,
        in_specs=[SM] * smem + [HB] * hbm + [VM] * (len(args) - smem - hbm),
        out_specs=VM if one else tuple(VM for _ in out_shape),
        scratch_shapes=list(scratch),
        compiler_params=pltpu.CompilerParams(vmem_limit_bytes=limit or (4 << 20)),
        cost_estimate=pl.CostEstimate(flops=flops, bytes_accessed=1 << 20, transcendentals=0),
    )(*args)


def shape(dims, dtype):
    return jax.ShapeDtypeStruct(tuple(dims), dtype)


MEMBERS = 4


def member():
    return lax.axis_index("ctx") % MEMBERS


def group_of():
    return lax.axis_index("ctx") // MEMBERS


def start_kernel(*refs):
    q_hbm, k_hbm, v_hbm, x_hbm, g_hbm, w_hbm, len_hbm, *refs = refs
    x_ref, g_ref, w_ref, total_ref, edge_ref, *refs = refs
    slots, (q_ref, k_ref, v_ref, len_ref, buf, sems) = refs[:-6], refs[-6:]
    rows, width = q_ref.shape
    half = rows // 2
    moves = (
        (x_hbm, x_ref),
        (g_hbm, g_ref),
        (k_hbm, k_ref),
        (v_hbm, v_ref),
        (q_hbm, q_ref),
        (w_hbm, w_ref),
        (len_hbm, len_ref),
    )
    copies = [pltpu.make_async_copy(a, b, sems.at[i]) for i, (a, b) in enumerate(moves)]
    for copy in copies:
        copy.start()
    for copy in copies:
        copy.wait()
    total = len_ref[0]
    for i in range(1, len_ref.shape[0]):
        total = total + len_ref[i]
    total_ref[...] = jnp.full(total_ref.shape, total, jnp.int32)
    for m in range(MEMBERS):
        cols = slice(m * HEAD_DIM, (m + 1) * HEAD_DIM)
        buf[m, 0:rows, 0:HEAD_DIM] = k_ref[:, cols]
        buf[m, 0:rows, HEAD_DIM:] = v_ref[:, cols]
        buf[m, rows:, 0:HEAD_DIM] = q_ref[0:half, cols]
        buf[m, rows:, HEAD_DIM:] = q_ref[half:, cols]
    me = member()
    for k in range(MEMBERS):
        slots[k][0 : rows + half] = buf[me ^ k]
    for ref, at, upward in (
        (slots[1], rows + half, me % 2 == 0),
        (slots[3], rows + half, me == 1),
        (edge_ref, 0, me == MEMBERS - 1),
    ):
        for c in range(width // 128):
            cols = slice(c * 128, (c + 1) * 128)
            for first, count, src in ((0, HALO_X, x_ref), (HALO_X, HALO_G, g_ref)):
                last = src[rows - count :, cols].astype(F32)
                chosen = jnp.where(upward, last, src[0:count, cols].astype(F32))
                to = at + c * (HALO_X + HALO_G) + first
                ref[to : to + count] = chosen.astype(BF)


def join_kernel(*refs):
    out_ref = refs[-1]
    rows = out_ref.shape[0] // MEMBERS
    for k, ref in enumerate(refs[:-1]):
        out_ref[k * rows : (k + 1) * rows] = ref[0:rows]


def conv_kernel(
    total_ref,
    x_ref,
    g_ref,
    w_ref,
    one_ref,
    three_ref,
    edge_ref,
    out_ref,
    send_ref,
    mine_ref,
    xs,
    gs,
):
    rows = x_ref.shape[0]
    taps = w_ref.shape[0]
    half = taps // 2
    wide = rows + 2 * HALO_G
    shift = HALO_X - HALO_G - half
    size = edge_ref.shape[0]
    start = one_ref.shape[0] - size
    me = member()
    one, three, edge = (
        one_ref[start:].astype(F32),
        three_ref[start:].astype(F32),
        edge_ref[...].astype(F32),
    )
    low = jnp.where(me == 0, edge, jnp.where(me == 2, three, one))
    high = jnp.where(me == 3, edge, jnp.where(me == 1, three, one))
    first = lax.axis_index("ctx") * rows
    for c in range(xs.shape[0]):
        cols = slice(c * 128, (c + 1) * 128)
        at = c * (HALO_X + HALO_G)
        xs[c, 0:HALO_X] = low[at : at + HALO_X]
        xs[c, HALO_X : HALO_X + rows] = x_ref[:, cols].astype(F32)
        xs[c, HALO_X + rows :] = high[at : at + HALO_X]
        pos = first - HALO_X + lax.broadcasted_iota(jnp.int32, xs.shape[1:], 0)
        xs[c] = jnp.where(pos < total_ref[0:1], xs[c], 0.0)
        w = w_ref[:, cols].astype(F32)
        acc = jnp.zeros((wide, 128), F32)
        for j in range(taps):
            acc = acc + w[j : j + 1] * xs[c, shift + j : shift + j + wide]
        s = jax.nn.sigmoid(acc)
        slope = s * (1.0 + acc * (1.0 - s))
        gs[c, 0:HALO_G] = low[at + HALO_X : at + HALO_X + HALO_G]
        gs[c, HALO_G : HALO_G + rows] = g_ref[:, cols].astype(F32)
        gs[c, HALO_G + rows :] = high[at + HALO_X : at + HALO_X + HALO_G]
        gs[c] = (gs[c] * slope).astype(BF).astype(F32)
        acc = jnp.zeros((rows, 128), F32)
        for j in range(taps):
            to = HALO_G + half - j
            acc = acc + w[j : j + 1] * gs[c, to : to + rows]
        pos = first + lax.broadcasted_iota(jnp.int32, acc.shape, 0)
        acc = jnp.where(pos < total_ref[0:1], acc, 0.0)
        out = (g_ref[:, cols].astype(F32) + acc).astype(BF)
        out_ref[:, cols] = out
        send_ref[:, cols] = out
        mine_ref[:, cols] = gs[c, HALO_G : HALO_G + rows].astype(BF)


def taps_kernel(taps, xs, mine_ref, after_ref, tap_ref):
    rows = mine_ref.shape[0]
    half = taps // 2
    sides = xs.shape[0]
    tap_rows = tap_ref.shape[0] // sides
    for c in range(sides):
        mine = mine_ref[:, c * 128 : (c + 1) * 128].astype(F32)
        sums = []
        for j in range(taps):
            first = HALO_X - half + j
            sums.append(jnp.sum(mine * xs[c, first : first + rows], axis=0, keepdims=True))
        sums.append(jnp.zeros((tap_rows - taps, 128), F32))
        tap_ref[c * tap_rows : (c + 1) * tap_rows] = jnp.concatenate(sums, 0).astype(BF)


def spread_kernel(pieces, proj_ref, *rest):
    n_heads = len(rest) - MEMBERS - 2
    xs, slots, (full, buf) = rest[:n_heads], rest[n_heads:-2], rest[-2:]
    rows, width = xs[0].shape
    half = rows // 2
    mine = lax.axis_index("head")
    for k in range(n_heads):
        full[mine ^ k] = xs[k][...]
    go = jnp.zeros((rows, proj_ref.shape[1]), F32)
    for b in range(n_heads):
        go = go + dot(full[b], proj_ref[b * width : (b + 1) * width], ((1,), (0,)))
    go = go.astype(BF)
    for m in range(MEMBERS):
        cols = slice(m * HEAD_DIM, (m + 1) * HEAD_DIM)
        buf[m, 0:half, 0:HEAD_DIM] = go[0:half, cols]
        buf[m, 0:half, HEAD_DIM:] = go[half:, cols]
        for i, first in enumerate(pieces[m]):
            buf[m, half + i * rows : half + (i + 1) * rows] = full[first // width][
                :, first % width : first % width + 128
            ]
    me = member()
    for k in range(MEMBERS):
        slots[k][...] = buf[me ^ k]


def widened(x, keep_high):
    x = x.astype(F32)
    turned = pltpu.roll(x, HEAD_DIM, 1)
    lane = lax.broadcasted_iota(jnp.int32, x.shape, 1)
    used = (lane >= HEAD_DIM) if keep_high else (lane < HEAD_DIM)
    first, second = (turned, x) if keep_high else (x, turned)
    return jnp.concatenate([jnp.where(used, first, 0.0), jnp.where(used, second, 0.0)], 0)


def over(count, body):
    if count <= 2:
        for g in range(count):
            body(g)
    else:
        lax.fori_loop(0, count, lambda g, c: (body(g), c)[1], 0)


def key_block(refs, g):
    return refs[0][g] if len(refs) == 1 else refs[g][...]


def queries_of(got_refs, scale):
    rows = got_refs[0].shape[0] * 2 // 3
    q = jnp.concatenate([r[rows : rows + rows // 2, :] for r in got_refs], 0)
    return (widened(q, False) * scale).astype(BF)


def forward_kernel(n_keys, scale, total_ref, tap_ref, *rest):
    got, rest = rest[:MEMBERS], rest[MEMBERS:]
    kv, rest = rest[:n_keys], rest[n_keys:]
    p_ref, slot_ref, s_ref, m_ref, l_ref, acc_ref = rest
    groups, keys, queries = s_ref.shape
    rows = keys // MEMBERS
    total = jnp.concatenate([total_ref[0:1]] * (queries // 128), 1)
    me, group = member(), group_of()
    q = queries_of(got, scale)
    m_ref[...] = jnp.full(m_ref.shape, -1e30, F32)
    l_ref[...] = jnp.zeros(l_ref.shape, F32)
    acc_ref[...] = jnp.zeros(acc_ref.shape, F32)

    def scores(g):
        s = dot(key_block(kv, g), q, ((1,), (1,)))
        from_group = lax.rem(group + g, groups) if n_keys > 1 else g
        for k in range(MEMBERS):
            start = (from_group * MEMBERS + (me ^ k)) * rows
            pos = start + lax.broadcasted_iota(jnp.int32, (rows, queries), 0)
            part = slice(k * rows, (k + 1) * rows)
            s_ref[g, part] = jnp.where(pos < total, s[part], -1e30)
        m_ref[...] = jnp.maximum(m_ref[...], jnp.max(s_ref[g], axis=0, keepdims=True))

    over(groups, scores)

    def weights(g):
        e = jnp.exp(s_ref[g] - m_ref[...])
        s_ref[g] = e
        l_ref[...] += jnp.sum(e, axis=0, keepdims=True)

    over(groups, weights)
    l_ref[...] = 1.0 / l_ref[...]

    def values(g):
        p = (s_ref[g] * l_ref[...]).astype(BF)
        p_ref[g] = p
        acc_ref[...] += dot(key_block(kv, g), p, ((0,), (0,)))

    over(groups, values)
    attn = acc_ref[HEAD_DIM:, :].T.astype(BF)
    half = queries // 2
    slot_ref[0:half, 0:HEAD_DIM] = attn[0:half]
    slot_ref[0:half, HEAD_DIM:] = attn[half:]
    slot_ref[half:] = tap_ref[...]


HALVES = ((1, 3), (0, 2))


def backward_kernel(n_keys, scale, p_ref, *rest):
    got, gos, rest = rest[:MEMBERS], rest[MEMBERS : 2 * MEMBERS], rest[2 * MEMBERS :]
    kv, rest = rest[:n_keys], rest[n_keys:]
    dkv, (dq_ref, s_ref, d_ref, acc_ref) = rest[:-4], rest[-4:]
    groups, keys, queries = s_ref.shape
    q = queries_of(got, scale)
    half = queries // MEMBERS // 2
    go = widened(jnp.concatenate([r[0:half] for r in gos], 0), True).astype(BF)
    d_ref[...] = jnp.zeros(d_ref.shape, F32)
    acc_ref[...] = jnp.zeros(acc_ref.shape, F32)

    def slopes(g):
        s = dot(key_block(kv, g), go, ((1,), (1,)))
        s_ref[g] = s
        d_ref[...] += jnp.sum(s * p_ref[g].astype(F32), axis=0, keepdims=True)

    over(groups, slopes)

    def grads(g):
        p = p_ref[g]
        ds = (p.astype(F32) * (s_ref[g] - d_ref[...])).astype(BF)
        acc_ref[...] += dot(key_block(kv, g), ds, ((0,), (0,)))
        out = (dot(ds, q, ((1,), (0,))) + dot(p, go, ((1,), (0,)))).astype(BF)
        if len(dkv) == 1:
            dkv[0][g] = out
        elif g == 0:
            dkv[0][...] = out
        else:
            rows = keys // MEMBERS
            for half, ref in zip(HALVES, dkv[1:]):
                for i, k in enumerate(half):
                    ref[i * rows : (i + 1) * rows] = out[k * rows : (k + 1) * rows]

    over(groups, grads)
    dq = (acc_ref[0:HEAD_DIM, :] * scale).T.astype(BF)
    half = queries // 2
    dq_ref[:, 0:HEAD_DIM] = dq[0:half]
    dq_ref[:, HEAD_DIM:] = dq[half:]


def project_kernel(own_rows, *refs):
    gos, slots, outs = refs[:MEMBERS], refs[MEMBERS : 2 * MEMBERS], refs[2 * MEMBERS : -3]
    out_ref, tap_ref = outs[:2]
    lhs, rhs, heads = refs[-3:]
    members = MEMBERS
    count, width = lhs.shape[1], rhs.shape[1]
    half = lhs.shape[0] // members
    rows = 2 * half
    me = member()
    acc = jnp.zeros((count, width), F32)
    tap = jnp.zeros(tap_ref.shape, F32)
    for k in range(members):
        heads[me ^ k] = slots[k][0 : members * half]
        tap = tap + slots[k][members * half :].astype(F32)
    tap_ref[...] = tap.astype(BF)
    for fold in range(2):
        for k in range(members):
            for side in range(count // 128):
                at = half + side * rows + fold * half
                where = pl.multiple_of((me ^ k) * half, half)
                lhs[pl.ds(where, half), side * 128 : (side + 1) * 128] = gos[k][at : at + half]
        for h in range(members):
            for i in range(members):
                j = h ^ i
                rhs[i * half : (i + 1) * half, h * HEAD_DIM : (h + 1) * HEAD_DIM] = heads[
                    h, j * half : (j + 1) * half, fold * HEAD_DIM : (fold + 1) * HEAD_DIM
                ]
        acc = acc + dot(lhs[...], rhs[...], ((0,), (0,)))
    if len(outs) == 2:
        out_ref[...] = acc
        return
    send_ref = outs[2]
    first = group_of() == 0
    low, high = acc[:own_rows], acc[own_rows:]
    out_ref[...] = jnp.where(first, low, high)
    theirs = jnp.where(first, high, low).astype(BF)
    for side in range(width // 128):
        send_ref[side * own_rows : (side + 1) * own_rows] = theirs[:, side * 128 : (side + 1) * 128]
    send_ref[width // 128 * own_rows :] = tap.astype(BF)


def collect_kernel(blocks, own_ref, *refs):
    slots, refs = refs[-len(blocks) :], refs[: -len(blocks)]
    dq_ref = refs[-1]
    rows = slots[0].shape[0] * 2 // 3
    half = rows // 2
    for i, (k, slot) in enumerate(zip(blocks, slots)):
        total = own_ref[k * rows : (k + 1) * rows]
        if len(refs) == 2:
            theirs = refs[0][i * rows : (i + 1) * rows].astype(F32)
            total = (total.astype(F32) + theirs).astype(BF)
        slot[0:rows] = total
        slot[rows:] = dq_ref[k * half : (k + 1) * half]


def end_kernel(*refs):
    n = MEMBERS
    finish_kernel(*refs[n : n + 3], *refs[-3:-1])
    unpack_kernel(*refs[:n], *refs[n + 3 : n + 6], refs[-1])


def unpack_kernel(*refs):
    slots, (q_ref, k_ref, v_ref, buf) = refs[:-4], refs[-4:]
    members = MEMBERS
    rows = q_ref.shape[0]
    half = rows // 2
    me = member()
    for k in range(members):
        buf[me ^ k] = slots[k][...]
    for m in range(members):
        cols = slice(m * HEAD_DIM, (m + 1) * HEAD_DIM)
        k_ref[:, cols] = buf[m, 0:rows, 0:HEAD_DIM]
        v_ref[:, cols] = buf[m, 0:rows, HEAD_DIM:]
        q_ref[0:half, cols] = buf[m, rows:, 0:HEAD_DIM]
        q_ref[half:, cols] = buf[m, rows:, HEAD_DIM:]


def finish_kernel(mine_ref, tap_ref, got_ref, out_ref, grad_ref):
    own_rows, width = mine_ref.shape
    taps = grad_ref.shape[0]
    sides = width // 128
    tap_rows = tap_ref.shape[0] // sides
    tap = tap_ref[...].astype(F32) + got_ref[sides * own_rows :].astype(F32)
    for side in range(sides):
        cols = slice(side * 128, (side + 1) * 128)
        out_ref[:, cols] = mine_ref[:, cols] + got_ref[
            side * own_rows : (side + 1) * own_rows
        ].astype(F32)
        grad_ref[:, cols] = tap[side * tap_rows : side * tap_rows + taps]


def on_device(
    query_all, key_all, value_all, cotangent, conv_input, rec_lengths, out_proj, conv_weight
):
    rows, width = query_all.shape
    half = rows // 2
    members = width // HEAD_DIM
    if members != MEMBERS:
        raise ValueError(width)
    n_ctx, n_heads = lax.axis_size("ctx"), lax.axis_size("head")
    groups = n_ctx // members
    channels = out_proj.shape[0]
    own_rows = channels // n_ctx
    scale = HEAD_DIM**-0.5
    taps = conv_weight.shape[0]
    tap_rows = -(-taps // 16) * 16
    sides = width // 128
    keys = members * rows
    queries = members * rows
    pair = groups == 2
    across = [[g * members + m for g in range(groups)] for m in range(members)]
    other = [(i, (i + members) % n_ctx) for i in range(n_ctx)]

    def move(x, pairs, axis="ctx"):
        return lax.ppermute(x, axis, pairs)

    def by_xor(x, k, axis="ctx"):
        return move(x, [(i, i ^ k) for i in range(lax.axis_size(axis))], axis)

    def swap(slots):
        return [slots[0]] + [by_xor(slots[k], k) for k in range(1, members)]

    edge_rows = sides * (HALO_X + HALO_G)
    given = (query_all, key_all, value_all, conv_input, cotangent, conv_weight, rec_lengths)
    x_in, g_in, w_in, total, edge, *slots = call(
        start_kernel,
        (
            shape((rows, width), BF),
            shape((rows, width), BF),
            shape(conv_weight.shape, BF),
            shape((8, 128), jnp.int32),
            shape((edge_rows, 128), BF),
        )
        + tuple(shape((rows + half + k % 2 * edge_rows, 128), BF) for k in range(members)),
        tuple(pltpu.with_memory_space_constraint(x, pltpu.HBM) for x in given),
        hbm=len(given),
        scratch=[pltpu.VMEM((rows, width), BF)] * 3
        + [
            pltpu.SMEM(rec_lengths.shape, jnp.int32),
            pltpu.VMEM((members, rows + half, 128), BF),
            pltpu.SemaphoreType.DMA((len(given),)),
        ],
    )
    got = swap(slots)
    borders = [i for i in range(members, n_ctx, members)]
    edge = move(edge, [(i - 1, i) for i in borders] + [(i, i - 1) for i in borders])
    x_grad, x_send, grad_conv, masked = call(
        conv_kernel,
        (shape((rows, width), BF),) * 3 + (shape((sides, rows + 2 * HALO_X, 128), F32),),
        (total, x_in, g_in, w_in, got[1], got[3], edge),
        scratch=[pltpu.VMEM((sides, rows + 2 * HALO_G, 128), F32)],
    )
    xs = [x_send] + [by_xor(x_send, k, "head") for k in range(1, n_heads)]
    own_kv = call(join_kernel, shape((keys, 128), BF), got)
    if pair:
        kv = (own_kv, move(own_kv, other))
    else:
        kv = (lax.all_gather(own_kv, "ctx", axis_index_groups=across),)
    n_keys = len(kv)
    count = groups * own_rows
    aligned = own_rows % 128 == 0
    pieces = [
        [(g * members + m) * own_rows + b for g in range(groups) for b in range(0, own_rows, 128)]
        if aligned
        else list(range(m * count, (m + 1) * count, 128))
        for m in range(members)
    ]
    slot_rows = half + count // 128 * rows
    spread = call(
        functools.partial(spread_kernel, pieces),
        (shape((slot_rows, 128), BF),) * members,
        (out_proj, *xs),
        scratch=[
            pltpu.VMEM((n_heads, rows, width), BF),
            pltpu.VMEM((members, slot_rows, 128), BF),
        ],
        flops=2 * rows * channels * width,
    )
    gos = swap(spread)
    tap_part = call(
        functools.partial(taps_kernel, taps),
        shape((sides * tap_rows, 128), BF),
        (masked, grad_conv, spread[0]),
    )
    big = (12 << 20) if groups <= 2 else (60 << 20)
    flops = 2 * queries * keys * groups * 128
    fwd = call(
        functools.partial(forward_kernel, n_keys, scale),
        (
            shape((groups, keys, queries), BF),
            shape((queries // 2 + sides * tap_rows, 128), BF),
        ),
        (total, tap_part, *got, *kv),
        scratch=[
            pltpu.VMEM((groups, keys, queries), F32),
            pltpu.VMEM((1, queries), F32),
            pltpu.VMEM((1, queries), F32),
            pltpu.VMEM((128, queries), F32),
        ],
        flops=2 * flops,
        limit=big,
    )
    probs = fwd[0]
    bwd = call(
        functools.partial(backward_kernel, n_keys, scale),
        (
            (shape((keys, 128), BF), shape((keys // 2, 128), BF), shape((keys // 2, 128), BF))
            if pair
            else (shape((groups, keys, 128), BF),)
        )
        + (shape((queries // 2, 128), BF),),
        (probs, *got, *gos, *kv),
        scratch=[
            pltpu.VMEM((groups, keys, queries), F32),
            pltpu.VMEM((1, queries), F32),
            pltpu.VMEM((128, queries), F32),
        ],
        flops=4 * flops,
        limit=big,
    )
    dq = bwd[-1]
    slot = shape((rows + half, 128), BF)
    slots = [None] * members
    if pair:
        for i, blocks in enumerate(HALVES):
            theirs = move(bwd[1 + i], other)
            made = call(
                functools.partial(collect_kernel, blocks),
                (slot,) * len(blocks),
                (bwd[0], theirs, dq),
            )
            for k, one in zip(blocks, made):
                slots[k] = one
    else:
        moved = lax.all_to_all(bwd[0], "ctx", 0, 0, axis_index_groups=across)
        summed = jnp.sum(moved.astype(F32), 0).astype(BF)
        slots = call(
            functools.partial(collect_kernel, tuple(range(members))), (slot,) * members, (summed, dq)
        )
    back = swap(slots)
    shared = swap([fwd[1]] * members)
    merged = pair and own_rows % 16 == 0
    tap_shape = shape((sides * tap_rows, 128), BF)
    outs = (
        (shape((own_rows, width), F32), tap_shape, shape((sides * (own_rows + tap_rows), 128), BF))
        if merged
        else (shape((count, width), F32), tap_shape)
    )
    partial, tap_sum, *send = call(
        functools.partial(project_kernel, own_rows),
        outs,
        (*gos, *shared),
        scratch=[
            pltpu.VMEM((members * half, count), BF),
            pltpu.VMEM((members * half, width), BF),
            pltpu.VMEM((members, queries // 2, 128), BF),
        ],
        flops=2 * count * width * queries,
    )
    grads = (shape((rows, width), BF),) * 3
    buf = [pltpu.VMEM((members, rows + half, 128), BF)]
    if merged:
        q_grad, k_grad, v_grad, out_proj_grad, conv_weight_grad = call(
            end_kernel,
            grads + (shape((own_rows, width), F32), shape((taps, width), F32)),
            (*back, partial, tap_sum, move(send[0], other)),
            scratch=buf,
        )
    else:
        q_grad, k_grad, v_grad = call(unpack_kernel, grads, tuple(back), scratch=buf)
        if not aligned:
            wanted = partial.astype(BF).reshape(1, groups, own_rows, width)
            slots = jnp.zeros((members, groups, own_rows, width), BF)
            slots = lax.dynamic_update_slice(
                slots, wanted, (member(), 0, 0, 0)
            )
            moved = lax.all_to_all(slots.reshape(n_ctx, own_rows, width), "ctx", 0, 0)
        else:
            moved = lax.all_to_all(
                partial.astype(BF).reshape(groups, own_rows, width),
                "ctx",
                0,
                0,
                axis_index_groups=across,
            )
        out_proj_grad = jnp.sum(moved.astype(F32), 0)
        tap_all = jnp.sum(
            lax.all_gather(tap_sum, "ctx", axis_index_groups=across).astype(F32), 0
        ).reshape(sides, tap_rows, 128)
        conv_weight_grad = jnp.swapaxes(tap_all, 0, 1).reshape(tap_rows, width)[:taps]
    return (q_grad, k_grad, v_grad, x_grad, out_proj_grad, conv_weight_grad)


def solution(mesh):
    placed = (
        P("ctx", "head"),
        P("ctx", "head"),
        P("ctx", "head"),
        P("ctx", "head"),
        P("ctx", "head"),
        P(),
        P(None, "head"),
        P(None, "head"),
    )

    return jax.shard_map(
        on_device,
        mesh=mesh,
        in_specs=placed,
        out_specs=(
            P("ctx", "head"),
            P("ctx", "head"),
            P("ctx", "head"),
            P("ctx", "head"),
            P("ctx", "head"),
            P(None, "head"),
        ),
        check_vma=False,
    )
```

```python
import functools

import jax
import jax.numpy as jnp
from jax import lax
from jax.experimental import pallas as pl
from jax.experimental.pallas import tpu as pltpu
from jax.sharding import PartitionSpec as P


HEAD_DIM = 64
HALO_X = 32
HALO_G = 16
BF = jnp.bfloat16
F32 = jnp.float32
VM = pl.BlockSpec(memory_space=pltpu.VMEM)
HB = pl.BlockSpec(memory_space=pltpu.HBM)
SM = pl.BlockSpec(memory_space=pltpu.SMEM)


def dot(a, b, dims):
    return lax.dot_general(a, b, (dims, ((), ())), preferred_element_type=F32)


def call(kernel, out_shape, args, smem=0, hbm=0, scratch=(), flops=1 << 20, limit=None):
    one = not isinstance(out_shape, (tuple, list))
    return pl.pallas_call(
        kernel,
        out_shape=out_shape,
        in_specs=[SM] * smem + [HB] * hbm + [VM] * (len(args) - smem - hbm),
        out_specs=VM if one else tuple(VM for _ in out_shape),
        scratch_shapes=list(scratch),
        compiler_params=pltpu.CompilerParams(vmem_limit_bytes=limit or (4 << 20)),
        cost_estimate=pl.CostEstimate(flops=flops, bytes_accessed=1 << 20, transcendentals=0),
    )(*args)


def shape(dims, dtype):
    return jax.ShapeDtypeStruct(tuple(dims), dtype)


MEMBERS = 4


def member():
    return lax.axis_index("ctx") % MEMBERS


def group_of():
    return lax.axis_index("ctx") // MEMBERS


def start_kernel(*refs):
    q_hbm, k_hbm, v_hbm, x_hbm, g_hbm, w_hbm, len_hbm, *refs = refs
    x_ref, g_ref, w_ref, total_ref, edge_ref, *refs = refs
    slots, (q_ref, k_ref, v_ref, len_ref, buf, sems) = refs[:-6], refs[-6:]
    rows, width = q_ref.shape
    half = rows // 2
    moves = (
        (x_hbm, x_ref),
        (g_hbm, g_ref),
        (k_hbm, k_ref),
        (v_hbm, v_ref),
        (q_hbm, q_ref),
        (w_hbm, w_ref),
        (len_hbm, len_ref),
    )
    copies = [pltpu.make_async_copy(a, b, sems.at[i]) for i, (a, b) in enumerate(moves)]
    for copy in copies:
        copy.start()
    for copy in copies:
        copy.wait()
    total = len_ref[0]
    for i in range(1, len_ref.shape[0]):
        total = total + len_ref[i]
    total_ref[...] = jnp.full(total_ref.shape, total, jnp.int32)
    for m in range(MEMBERS):
        cols = slice(m * HEAD_DIM, (m + 1) * HEAD_DIM)
        buf[m, 0:rows, 0:HEAD_DIM] = k_ref[:, cols]
        buf[m, 0:rows, HEAD_DIM:] = v_ref[:, cols]
        buf[m, rows:, 0:HEAD_DIM] = q_ref[0:half, cols]
        buf[m, rows:, HEAD_DIM:] = q_ref[half:, cols]
    me = member()
    for k in range(MEMBERS):
        slots[k][0 : rows + half] = buf[me ^ k]
    for ref, at, upward in (
        (slots[1], rows + half, me % 2 == 0),
        (slots[3], rows + half, me == 1),
        (edge_ref, 0, me == MEMBERS - 1),
    ):
        for c in range(width // 128):
            cols = slice(c * 128, (c + 1) * 128)
            for first, count, src in ((0, HALO_X, x_ref), (HALO_X, HALO_G, g_ref)):
                last = src[rows - count :, cols].astype(F32)
                chosen = jnp.where(upward, last, src[0:count, cols].astype(F32))
                to = at + c * (HALO_X + HALO_G) + first
                ref[to : to + count] = chosen.astype(BF)


def join_kernel(*refs):
    out_ref = refs[-1]
    rows = out_ref.shape[0] // MEMBERS
    for k, ref in enumerate(refs[:-1]):
        out_ref[k * rows : (k + 1) * rows] = ref[0:rows]


def slope_of(acc):
    s = jax.nn.sigmoid(acc)
    return s * (1.0 + acc * (1.0 - s))


def window(w, ref, c, first, count, step):
    acc = jnp.zeros((count, 128), F32)
    for j in range(w.shape[0]):
        at = first + step * j
        acc = acc + w[j : j + 1] * ref[c, at : at + count]
    return acc


def interior_kernel(total_ref, x_ref, g_ref, w_ref, after_ref, xs, gs, sums):
    rows = x_ref.shape[0]
    half = w_ref.shape[0] // 2
    shift = HALO_X - HALO_G - half
    inner = 2 * HALO_G
    first = lax.axis_index("ctx") * rows
    for c in range(xs.shape[0]):
        cols = slice(c * 128, (c + 1) * 128)
        own = slice(HALO_X, HALO_X + rows)
        pos = first + lax.broadcasted_iota(jnp.int32, (rows, 128), 0)
        xs[c, own] = jnp.where(pos < total_ref[0:1], x_ref[:, cols].astype(F32), 0.0)
        w = w_ref[:, cols].astype(F32)
        slope = slope_of(window(w, xs, c, shift + inner, rows - inner, 1))
        grad = g_ref[HALO_G : rows - HALO_G, cols].astype(F32) * slope
        gs[c, inner:rows] = grad.astype(BF).astype(F32)
        sums[c] = window(w, gs, c, inner + HALO_G + half, rows - 2 * inner, -1)


def conv_kernel(
    total_ref,
    g_ref,
    w_ref,
    one_ref,
    three_ref,
    edge_ref,
    xs_in,
    gs_in,
    sums,
    out_ref,
    send_ref,
    mine_ref,
    xs,
    gs,
):
    rows = g_ref.shape[0]
    half = w_ref.shape[0] // 2
    shift = HALO_X - HALO_G - half
    inner = 2 * HALO_G
    start = one_ref.shape[0] - edge_ref.shape[0]
    me = member()
    one, three, edge = (
        one_ref[start:].astype(F32),
        three_ref[start:].astype(F32),
        edge_ref[...].astype(F32),
    )
    low = jnp.where(me == 0, edge, jnp.where(me == 2, three, one))
    high = jnp.where(me == 3, edge, jnp.where(me == 1, three, one))
    first = lax.axis_index("ctx") * rows
    total = total_ref[0:1]
    for c in range(xs.shape[0]):
        cols = slice(c * 128, (c + 1) * 128)
        at = c * (HALO_X + HALO_G)
        step = lax.broadcasted_iota(jnp.int32, (HALO_X, 128), 0)
        xs[c, 0:HALO_X] = jnp.where(first - HALO_X + step < total, low[at : at + HALO_X], 0.0)
        xs[c, HALO_X : HALO_X + rows] = xs_in[c, HALO_X : HALO_X + rows]
        xs[c, HALO_X + rows :] = jnp.where(first + rows + step < total, high[at : at + HALO_X], 0.0)
        w = w_ref[:, cols].astype(F32)
        gs[c, inner:rows] = gs_in[c, inner:rows]
        g_low = low[at + HALO_X : at + HALO_X + HALO_G]
        g_high = high[at + HALO_X : at + HALO_X + HALO_G]
        for to, parts in (
            (0, (g_low, g_ref[0:HALO_G, cols].astype(F32))),
            (rows, (g_ref[rows - HALO_G :, cols].astype(F32), g_high)),
        ):
            slope = slope_of(window(w, xs, c, shift + to, inner, 1))
            grad = jnp.concatenate(parts, 0) * slope
            gs[c, to : to + inner] = grad.astype(BF).astype(F32)
        acc = jnp.concatenate(
            [
                window(w, gs, c, HALO_G + half, inner, -1),
                sums[c],
                window(w, gs, c, rows - inner + HALO_G + half, inner, -1),
            ],
            0,
        )
        pos = first + lax.broadcasted_iota(jnp.int32, acc.shape, 0)
        acc = jnp.where(pos < total, acc, 0.0)
        out = (g_ref[:, cols].astype(F32) + acc).astype(BF)
        out_ref[:, cols] = out
        send_ref[:, cols] = out
        mine_ref[:, cols] = gs[c, HALO_G : HALO_G + rows].astype(BF)


def taps_kernel(taps, xs, mine_ref, after_ref, tap_ref):
    rows = mine_ref.shape[0]
    half = taps // 2
    sides = xs.shape[0]
    tap_rows = tap_ref.shape[0] // sides
    for c in range(sides):
        mine = mine_ref[:, c * 128 : (c + 1) * 128].astype(F32)
        sums = []
        for j in range(taps):
            first = HALO_X - half + j
            sums.append(jnp.sum(mine * xs[c, first : first + rows], axis=0, keepdims=True))
        sums.append(jnp.zeros((tap_rows - taps, 128), F32))
        tap_ref[c * tap_rows : (c + 1) * tap_rows] = jnp.concatenate(sums, 0).astype(BF)


def spread_kernel(pieces, proj_ref, *rest):
    n_heads = len(rest) - MEMBERS - 2
    xs, slots, (full, buf) = rest[:n_heads], rest[n_heads:-2], rest[-2:]
    rows, width = xs[0].shape
    half = rows // 2
    mine = lax.axis_index("head")
    for k in range(n_heads):
        full[mine ^ k] = xs[k][...]
    go = jnp.zeros((rows, proj_ref.shape[1]), F32)
    for b in range(n_heads):
        go = go + dot(full[b], proj_ref[b * width : (b + 1) * width], ((1,), (0,)))
    go = go.astype(BF)
    for m in range(MEMBERS):
        cols = slice(m * HEAD_DIM, (m + 1) * HEAD_DIM)
        buf[m, 0:half, 0:HEAD_DIM] = go[0:half, cols]
        buf[m, 0:half, HEAD_DIM:] = go[half:, cols]
        for i, first in enumerate(pieces[m]):
            buf[m, half + i * rows : half + (i + 1) * rows] = full[first // width][
                :, first % width : first % width + 128
            ]
    me = member()
    for k in range(MEMBERS):
        slots[k][...] = buf[me ^ k]


def widened(x, keep_high):
    x = x.astype(F32)
    turned = pltpu.roll(x, HEAD_DIM, 1)
    lane = lax.broadcasted_iota(jnp.int32, x.shape, 1)
    used = (lane >= HEAD_DIM) if keep_high else (lane < HEAD_DIM)
    first, second = (turned, x) if keep_high else (x, turned)
    return jnp.concatenate([jnp.where(used, first, 0.0), jnp.where(used, second, 0.0)], 0)


def over(count, body):
    if count <= 2:
        for g in range(count):
            body(g)
    else:
        lax.fori_loop(0, count, lambda g, c: (body(g), c)[1], 0)


def key_block(refs, g):
    return refs[0][g] if len(refs) == 1 else refs[g][...]


def queries_of(got_refs, scale):
    rows = got_refs[0].shape[0] * 2 // 3
    q = jnp.concatenate([r[rows : rows + rows // 2, :] for r in got_refs], 0)
    return (widened(q, False) * scale).astype(BF)


def forward_kernel(n_keys, scale, total_ref, tap_ref, *rest):
    got, rest = rest[:MEMBERS], rest[MEMBERS:]
    kv, rest = rest[:n_keys], rest[n_keys:]
    p_ref, slot_ref, s_ref, m_ref, l_ref, acc_ref = rest
    groups, keys, queries = s_ref.shape
    rows = keys // MEMBERS
    total = jnp.concatenate([total_ref[0:1]] * (queries // 128), 1)
    me, group = member(), group_of()
    q = queries_of(got, scale)
    m_ref[...] = jnp.full(m_ref.shape, -1e30, F32)
    l_ref[...] = jnp.zeros(l_ref.shape, F32)
    acc_ref[...] = jnp.zeros(acc_ref.shape, F32)

    def scores(g):
        s = dot(key_block(kv, g), q, ((1,), (1,)))
        from_group = lax.rem(group + g, groups) if n_keys > 1 else g
        for k in range(MEMBERS):
            start = (from_group * MEMBERS + (me ^ k)) * rows
            pos = start + lax.broadcasted_iota(jnp.int32, (rows, queries), 0)
            part = slice(k * rows, (k + 1) * rows)
            s_ref[g, part] = jnp.where(pos < total, s[part], -1e30)
        m_ref[...] = jnp.maximum(m_ref[...], jnp.max(s_ref[g], axis=0, keepdims=True))

    over(groups, scores)

    def weights(g):
        e = jnp.exp(s_ref[g] - m_ref[...])
        s_ref[g] = e
        l_ref[...] += jnp.sum(e, axis=0, keepdims=True)

    over(groups, weights)
    l_ref[...] = 1.0 / l_ref[...]

    def values(g):
        p = (s_ref[g] * l_ref[...]).astype(BF)
        p_ref[g] = p
        acc_ref[...] += dot(key_block(kv, g), p, ((0,), (0,)))

    over(groups, values)
    attn = acc_ref[HEAD_DIM:, :].T.astype(BF)
    half = queries // 2
    slot_ref[0:half, 0:HEAD_DIM] = attn[0:half]
    slot_ref[0:half, HEAD_DIM:] = attn[half:]
    slot_ref[half:] = tap_ref[...]


HALVES = ((1, 3), (0, 2))


def backward_kernel(n_keys, scale, p_ref, *rest):
    got, gos, rest = rest[:MEMBERS], rest[MEMBERS : 2 * MEMBERS], rest[2 * MEMBERS :]
    kv, rest = rest[:n_keys], rest[n_keys:]
    dkv, (dq_ref, s_ref, d_ref, acc_ref) = rest[:-4], rest[-4:]
    groups, _, queries = s_ref.shape
    q = queries_of(got, scale)
    half = queries // MEMBERS // 2
    go = widened(jnp.concatenate([r[0:half] for r in gos], 0), True).astype(BF)
    d_ref[...] = jnp.zeros(d_ref.shape, F32)
    acc_ref[...] = jnp.zeros(acc_ref.shape, F32)

    def slopes(g):
        s = dot(key_block(kv, g), go, ((1,), (1,)))
        s_ref[g] = s
        d_ref[...] += jnp.sum(s * p_ref[g].astype(F32), axis=0, keepdims=True)

    over(groups, slopes)

    def grads(g):
        p = p_ref[g]
        ds = (p.astype(F32) * (s_ref[g] - d_ref[...])).astype(BF)
        acc_ref[...] += dot(key_block(kv, g), ds, ((0,), (0,)))
        out = (dot(ds, q, ((1,), (0,))) + dot(p, go, ((1,), (0,)))).astype(BF)
        dkv[0][g] = out

    over(groups, grads)
    dq = (acc_ref[0:HEAD_DIM, :] * scale).T.astype(BF)
    half = queries // 2
    dq_ref[:, 0:HEAD_DIM] = dq[0:half]
    dq_ref[:, HEAD_DIM:] = dq[half:]


def send_kernel(scale, p_ref, *rest):
    got, gos, rest = rest[:MEMBERS], rest[MEMBERS : 2 * MEMBERS], rest[2 * MEMBERS :]
    own_ref, other_ref, *dkv, s_ref, d_ref = rest
    _, keys, queries = s_ref.shape
    q = queries_of(got, scale)
    half = queries // MEMBERS // 2
    go = widened(jnp.concatenate([r[0:half] for r in gos], 0), True).astype(BF)
    delta = jnp.zeros((1, queries), F32)
    for g, kv in enumerate((own_ref, other_ref)):
        s = dot(kv[...], go, ((1,), (1,)))
        s_ref[g] = s
        delta = delta + jnp.sum(s * p_ref[g].astype(F32), axis=0, keepdims=True)
    d_ref[...] = jnp.broadcast_to(delta, d_ref.shape)
    p = p_ref[1]
    ds = (p.astype(F32) * (s_ref[1] - delta)).astype(BF)
    out = (dot(ds, q, ((1,), (0,))) + dot(p, go, ((1,), (0,)))).astype(BF)
    rows = keys // MEMBERS
    for blocks, ref in zip(HALVES, dkv):
        for i, k in enumerate(blocks):
            ref[i * rows : (i + 1) * rows] = out[k * rows : (k + 1) * rows]


def own_kernel(scale, p_ref, s_ref, d_ref, *rest):
    got, gos, rest = rest[:MEMBERS], rest[MEMBERS : 2 * MEMBERS], rest[2 * MEMBERS :]
    own_ref, other_ref, dkv_ref, dq_ref = rest
    queries = s_ref.shape[2]
    q = queries_of(got, scale)
    half = queries // MEMBERS // 2
    go = widened(jnp.concatenate([r[0:half] for r in gos], 0), True).astype(BF)
    acc = jnp.zeros((128, queries), F32)
    for g, kv in enumerate((own_ref, other_ref)):
        p = p_ref[g]
        ds = (p.astype(F32) * (s_ref[g] - d_ref[0:1])).astype(BF)
        acc = acc + dot(kv[...], ds, ((0,), (0,)))
        if g == 0:
            dkv_ref[...] = (dot(ds, q, ((1,), (0,))) + dot(p, go, ((1,), (0,)))).astype(BF)
    dq = (acc[0:HEAD_DIM, :] * scale).T.astype(BF)
    half = queries // 2
    dq_ref[:, 0:HEAD_DIM] = dq[0:half]
    dq_ref[:, HEAD_DIM:] = dq[half:]


def project_kernel(own_rows, *refs):
    gos, slots, outs = refs[:MEMBERS], refs[MEMBERS : 2 * MEMBERS], refs[2 * MEMBERS : -3]
    out_ref, tap_ref = outs[:2]
    lhs, rhs, heads = refs[-3:]
    members = MEMBERS
    count, width = lhs.shape[1], rhs.shape[1]
    half = lhs.shape[0] // members
    rows = 2 * half
    me = member()
    acc = jnp.zeros((count, width), F32)
    tap = jnp.zeros(tap_ref.shape, F32)
    for k in range(members):
        heads[me ^ k] = slots[k][0 : members * half]
        tap = tap + slots[k][members * half :].astype(F32)
    tap_ref[...] = tap.astype(BF)
    for fold in range(2):
        for k in range(members):
            for side in range(count // 128):
                at = half + side * rows + fold * half
                where = pl.multiple_of((me ^ k) * half, half)
                lhs[pl.ds(where, half), side * 128 : (side + 1) * 128] = gos[k][at : at + half]
        for h in range(members):
            for i in range(members):
                j = h ^ i
                rhs[i * half : (i + 1) * half, h * HEAD_DIM : (h + 1) * HEAD_DIM] = heads[
                    h, j * half : (j + 1) * half, fold * HEAD_DIM : (fold + 1) * HEAD_DIM
                ]
        acc = acc + dot(lhs[...], rhs[...], ((0,), (0,)))
    if len(outs) == 2:
        out_ref[...] = acc
        return
    send_ref = outs[2]
    first = group_of() == 0
    low, high = acc[:own_rows], acc[own_rows:]
    out_ref[...] = jnp.where(first, low, high)
    theirs = jnp.where(first, high, low).astype(BF)
    for side in range(width // 128):
        send_ref[side * own_rows : (side + 1) * own_rows] = theirs[:, side * 128 : (side + 1) * 128]
    send_ref[width // 128 * own_rows :] = tap.astype(BF)


def collect_kernel(blocks, own_ref, *refs):
    slots, refs = refs[-len(blocks) :], refs[: -len(blocks)]
    dq_ref = refs[-1]
    rows = slots[0].shape[0] * 2 // 3
    half = rows // 2
    for i, (k, slot) in enumerate(zip(blocks, slots)):
        total = own_ref[k * rows : (k + 1) * rows]
        if len(refs) == 2:
            theirs = refs[0][i * rows : (i + 1) * rows].astype(F32)
            total = (total.astype(F32) + theirs).astype(BF)
        slot[0:rows] = total
        slot[rows:] = dq_ref[k * half : (k + 1) * half]


def end_kernel(*refs):
    n = MEMBERS
    finish_kernel(*refs[n : n + 3], *refs[-3:-1])
    unpack_kernel(*refs[:n], *refs[n + 3 : n + 6], refs[-1])


def unpack_kernel(*refs):
    slots, (q_ref, k_ref, v_ref, buf) = refs[:-4], refs[-4:]
    members = MEMBERS
    rows = q_ref.shape[0]
    half = rows // 2
    me = member()
    for k in range(members):
        buf[me ^ k] = slots[k][...]
    for m in range(members):
        cols = slice(m * HEAD_DIM, (m + 1) * HEAD_DIM)
        k_ref[:, cols] = buf[m, 0:rows, 0:HEAD_DIM]
        v_ref[:, cols] = buf[m, 0:rows, HEAD_DIM:]
        q_ref[0:half, cols] = buf[m, rows:, 0:HEAD_DIM]
        q_ref[half:, cols] = buf[m, rows:, HEAD_DIM:]


def finish_kernel(mine_ref, tap_ref, got_ref, out_ref, grad_ref):
    own_rows, width = mine_ref.shape
    taps = grad_ref.shape[0]
    sides = width // 128
    tap_rows = tap_ref.shape[0] // sides
    tap = tap_ref[...].astype(F32) + got_ref[sides * own_rows :].astype(F32)
    for side in range(sides):
        cols = slice(side * 128, (side + 1) * 128)
        out_ref[:, cols] = mine_ref[:, cols] + got_ref[
            side * own_rows : (side + 1) * own_rows
        ].astype(F32)
        grad_ref[:, cols] = tap[side * tap_rows : side * tap_rows + taps]


def on_device(
    query_all, key_all, value_all, cotangent, conv_input, rec_lengths, out_proj, conv_weight
):
    rows, width = query_all.shape
    half = rows // 2
    members = width // HEAD_DIM
    if members != MEMBERS:
        raise ValueError(width)
    n_ctx, n_heads = lax.axis_size("ctx"), lax.axis_size("head")
    groups = n_ctx // members
    channels = out_proj.shape[0]
    own_rows = channels // n_ctx
    scale = HEAD_DIM**-0.5
    taps = conv_weight.shape[0]
    tap_rows = -(-taps // 16) * 16
    sides = width // 128
    keys = members * rows
    queries = members * rows
    pair = groups == 2
    across = [[g * members + m for g in range(groups)] for m in range(members)]
    other = [(i, (i + members) % n_ctx) for i in range(n_ctx)]

    def move(x, pairs, axis="ctx"):
        return lax.ppermute(x, axis, pairs)

    def by_xor(x, k, axis="ctx"):
        return move(x, [(i, i ^ k) for i in range(lax.axis_size(axis))], axis)

    def swap(slots):
        return [slots[0]] + [by_xor(slots[k], k) for k in range(1, members)]

    edge_rows = sides * (HALO_X + HALO_G)
    given = (query_all, key_all, value_all, conv_input, cotangent, conv_weight, rec_lengths)
    x_in, g_in, w_in, total, edge, *slots = call(
        start_kernel,
        (
            shape((rows, width), BF),
            shape((rows, width), BF),
            shape(conv_weight.shape, BF),
            shape((8, 128), jnp.int32),
            shape((edge_rows, 128), BF),
        )
        + tuple(shape((rows + half + k % 2 * edge_rows, 128), BF) for k in range(members)),
        tuple(pltpu.with_memory_space_constraint(x, pltpu.HBM) for x in given),
        hbm=len(given),
        scratch=[pltpu.VMEM((rows, width), BF)] * 3
        + [
            pltpu.SMEM(rec_lengths.shape, jnp.int32),
            pltpu.VMEM((members, rows + half, 128), BF),
            pltpu.SemaphoreType.DMA((len(given),)),
        ],
    )
    got = swap(slots)
    borders = [i for i in range(members, n_ctx, members)]
    edge = move(edge, [(i - 1, i) for i in borders] + [(i, i - 1) for i in borders])
    wide_x = shape((sides, rows + 2 * HALO_X, 128), F32)
    wide_g = shape((sides, rows + 2 * HALO_G, 128), F32)
    inside = call(
        interior_kernel,
        (wide_x, wide_g, shape((sides, rows - 4 * HALO_G, 128), F32)),
        (total, x_in, g_in, w_in, slots[2]),
    )
    x_grad, x_send, grad_conv, masked = call(
        conv_kernel,
        (shape((rows, width), BF),) * 3 + (wide_x,),
        (total, g_in, w_in, got[1], got[3], edge, *inside),
        scratch=[pltpu.VMEM(wide_g.shape, F32)],
    )
    xs = [x_send] + [by_xor(x_send, k, "head") for k in range(1, n_heads)]
    own_kv = call(join_kernel, shape((keys, 128), BF), got)
    if pair:
        kv = (own_kv, move(own_kv, other))
    else:
        kv = (lax.all_gather(own_kv, "ctx", axis_index_groups=across),)
    n_keys = len(kv)
    count = groups * own_rows
    aligned = own_rows % 128 == 0
    pieces = [
        [(g * members + m) * own_rows + b for g in range(groups) for b in range(0, own_rows, 128)]
        if aligned
        else list(range(m * count, (m + 1) * count, 128))
        for m in range(members)
    ]
    slot_rows = half + count // 128 * rows
    spread = call(
        functools.partial(spread_kernel, pieces),
        (shape((slot_rows, 128), BF),) * members,
        (out_proj, *xs),
        scratch=[
            pltpu.VMEM((n_heads, rows, width), BF),
            pltpu.VMEM((members, slot_rows, 128), BF),
        ],
        flops=2 * rows * channels * width,
    )
    gos = swap(spread)
    tap_part = call(
        functools.partial(taps_kernel, taps),
        shape((sides * tap_rows, 128), BF),
        (masked, grad_conv, spread[0]),
    )
    big = (12 << 20) if groups <= 2 else (60 << 20)
    flops = 2 * queries * keys * groups * 128
    fwd = call(
        functools.partial(forward_kernel, n_keys, scale),
        (
            shape((groups, keys, queries), BF),
            shape((queries // 2 + sides * tap_rows, 128), BF),
        ),
        (total, tap_part, *got, *kv),
        scratch=[
            pltpu.VMEM((groups, keys, queries), F32),
            pltpu.VMEM((1, queries), F32),
            pltpu.VMEM((1, queries), F32),
            pltpu.VMEM((128, queries), F32),
        ],
        flops=2 * flops,
        limit=big,
    )
    probs = fwd[0]
    if pair:
        *leaving, slopes, delta = call(
            functools.partial(send_kernel, scale),
            tuple(shape((len(h) * rows, 128), BF) for h in HALVES)
            + (shape((groups, keys, queries), F32), shape((8, queries), F32)),
            (probs, *got, *gos, *kv),
            flops=2 * flops,
            limit=big,
        )
        own, dq = call(
            functools.partial(own_kernel, scale),
            (shape((keys, 128), BF), shape((queries // 2, 128), BF)),
            (probs, slopes, delta, *got, *gos, *kv),
            flops=2 * flops,
            limit=big,
        )
        bwd = (own, *leaving)
    else:
        bwd = call(
            functools.partial(backward_kernel, n_keys, scale),
            (shape((groups, keys, 128), BF), shape((queries // 2, 128), BF)),
            (probs, *got, *gos, *kv),
            scratch=[
                pltpu.VMEM((groups, keys, queries), F32),
                pltpu.VMEM((1, queries), F32),
                pltpu.VMEM((128, queries), F32),
            ],
            flops=4 * flops,
            limit=big,
        )
        dq = bwd[1]
    slot = shape((rows + half, 128), BF)
    slots = [None] * members
    if pair:
        for i, blocks in enumerate(HALVES):
            theirs = move(bwd[1 + i], other)
            made = call(
                functools.partial(collect_kernel, blocks),
                (slot,) * len(blocks),
                (bwd[0], theirs, dq),
            )
            for k, one in zip(blocks, made):
                slots[k] = one
    else:
        moved = lax.all_to_all(bwd[0], "ctx", 0, 0, axis_index_groups=across)
        summed = jnp.sum(moved.astype(F32), 0).astype(BF)
        slots = call(
            functools.partial(collect_kernel, tuple(range(members))), (slot,) * members, (summed, dq)
        )
    back = swap(slots)
    shared = swap([fwd[1]] * members)
    merged = pair and own_rows % 16 == 0
    tap_shape = shape((sides * tap_rows, 128), BF)
    outs = (
        (shape((own_rows, width), F32), tap_shape, shape((sides * (own_rows + tap_rows), 128), BF))
        if merged
        else (shape((count, width), F32), tap_shape)
    )
    partial, tap_sum, *send = call(
        functools.partial(project_kernel, own_rows),
        outs,
        (*gos, *shared),
        scratch=[
            pltpu.VMEM((members * half, count), BF),
            pltpu.VMEM((members * half, width), BF),
            pltpu.VMEM((members, queries // 2, 128), BF),
        ],
        flops=2 * count * width * queries,
    )
    grads = (shape((rows, width), BF),) * 3
    buf = [pltpu.VMEM((members, rows + half, 128), BF)]
    if merged:
        q_grad, k_grad, v_grad, out_proj_grad, conv_weight_grad = call(
            end_kernel,
            grads + (shape((own_rows, width), F32), shape((taps, width), F32)),
            (*back, partial, tap_sum, move(send[0], other)),
            scratch=buf,
        )
    else:
        q_grad, k_grad, v_grad = call(unpack_kernel, grads, tuple(back), scratch=buf)
        if not aligned:
            wanted = partial.astype(BF).reshape(1, groups, own_rows, width)
            slots = jnp.zeros((members, groups, own_rows, width), BF)
            slots = lax.dynamic_update_slice(
                slots, wanted, (member(), 0, 0, 0)
            )
            moved = lax.all_to_all(slots.reshape(n_ctx, own_rows, width), "ctx", 0, 0)
        else:
            moved = lax.all_to_all(
                partial.astype(BF).reshape(groups, own_rows, width),
                "ctx",
                0,
                0,
                axis_index_groups=across,
            )
        out_proj_grad = jnp.sum(moved.astype(F32), 0)
        tap_all = jnp.sum(
            lax.all_gather(tap_sum, "ctx", axis_index_groups=across).astype(F32), 0
        ).reshape(sides, tap_rows, 128)
        conv_weight_grad = jnp.swapaxes(tap_all, 0, 1).reshape(tap_rows, width)[:taps]
    return (q_grad, k_grad, v_grad, x_grad, out_proj_grad, conv_weight_grad)


def solution(mesh):
    placed = (
        P("ctx", "head"),
        P("ctx", "head"),
        P("ctx", "head"),
        P("ctx", "head"),
        P("ctx", "head"),
        P(),
        P(None, "head"),
        P(None, "head"),
    )

    return jax.shard_map(
        on_device,
        mesh=mesh,
        in_specs=placed,
        out_specs=(
            P("ctx", "head"),
            P("ctx", "head"),
            P("ctx", "head"),
            P("ctx", "head"),
            P("ctx", "head"),
            P(None, "head"),
        ),
        check_vma=False,
    )
```
